32 devices in a mesh: tile: 32 (over z, y, x, core), lev: 1.
Axes of the slice: x: 2, y: 2, z: 4, core: 2. Of those that a mesh axis runs over, the one named last changes fastest.
Arguments:
- cotangent: float32 [24, 4, 64, 900], P('lev', None, 'tile'), may hold values from -6 to 6
- courant_x: float32 [24, 64, 900], P('lev', 'tile'), may hold values from -0.6 to 0.6
- courant_y: float32 [24, 64, 900], P('lev', 'tile'), may hold values from -0.6 to 0.6
- diffusivity: float32 [64, 900], P('tile'), may hold values from 0.04 to 0.16
- vert_diff: float32 [24, 64, 900], P('lev', 'tile'), may hold values from 0.5 to 2000
- level_count: int32 [64, 900], P('tile'), may hold values from 0 to 24
- edge_tile: int32 [64, 4], P('tile'), may hold values from -1 to 63, as said below
- edge_code: int32 [64, 4], P('tile'), may hold values from 0 to 7
- corner_tile: int32 [64, 4], P('tile'), may hold values from -1 to 63, as said below
- corner_code: int32 [64, 4], P('tile'), may hold values from 0 to 3
Outputs:
- tracer_adjoint: float32 [24, 4, 64, 900], P('lev', None, 'tile')
The draws below stay inside these ranges and needn't reach their ends.
Inputs may be any that keep to these rules, and one draw needn't show every extreme that they name: Side lists are symmetric: if edge_tile[t, s] = q and edge_code[t, s] = e + 4 r, then edge_tile[q, e] = t and edge_code[q, e] = s + 4 r. Every partner q satisfies min(|q - t|, 64 - |q - t|) <= 16. Sides at the band's rim and sides towards land are -1. Corner lists are symmetric: if corner_tile[t, c] = q and corner_code[t, c] = k, then corner_tile[q, k] = t and corner_code[q, k] = c. Every partner q satisfies min(|q - t|, 64 - |q - t|) <= 16.
All inputs are finite; a program needn't handle non-finite values.
Results may differ from the reference program's by a relative error of at most 0.0003.
Values sent between devices are 32-bit elements; how exact they have to be, the bound alone decides.
A program may use at most 128 MiB of HBM per device.

```python
import math
import jax
import jax.numpy as jnp
from jax import lax

EDGE = 30
CELLS = 900
TRACERS = 4
LEV_DEV = 24
LEVELS = 24
TILES = 64
BAND = 8
ALONG = 10
LAND = 16


def build_lists(key):
    folded = jax.random.fold_in(key, 7)
    key_land, key_seam = jax.random.split(folded)
    positions = ALONG * BAND
    shuffled = jax.random.permutation(key_land, positions)
    land_flag = jnp.zeros((positions,), jnp.int32).at[shuffled[:LAND]].set(1)
    wet_index = jnp.where(land_flag == 0, jnp.cumsum(1 - land_flag) - 1, -1).astype(jnp.int32)
    wet_place = jnp.argsort(land_flag, stable=True)[:TILES].astype(jnp.int32)
    column = wet_place // BAND
    across = wet_place % BAND
    seam_flags = jax.random.randint(key_seam, (ALONG,), 0, 2).astype(jnp.int32)

    def lookup(column_to, across_to, inside):
        grid_spot = column_to % ALONG * BAND + jnp.clip(across_to, 0, BAND - 1)
        wet_found = wet_index[grid_spot]
        return jnp.where(inside & (wet_found >= 0), wet_found, -1).astype(jnp.int32)
    always = across >= 0
    south_tile = lookup(column, across - 1, across > 0)
    north_tile = lookup(column, across + 1, across < BAND - 1)
    west_seam = seam_flags[(column - 1) % ALONG]
    west_tile = lookup(column - 1, jnp.where(west_seam == 1, BAND - 1 - across, across), always)
    east_seam = seam_flags[column % ALONG]
    east_tile = lookup(column + 1, jnp.where(east_seam == 1, BAND - 1 - across, across), always)
    edge_tiles = jnp.stack([south_tile, north_tile, west_tile, east_tile], axis=1)
    edge_codes = jnp.stack([jnp.ones_like(across), jnp.zeros_like(across), 3 + 4 * west_seam, 2 + 4 * east_seam], axis=1).astype(jnp.int32)
    corner_tiles = []
    corner_codes = []
    for corner_slot in range(4):
        row_bit = corner_slot // 2
        col_bit = corner_slot % 2
        seam_here = seam_flags[(column + col_bit - 1) % ALONG]
        target = across + 2 * row_bit - 1
        inside = (target >= 0) & (target < BAND)
        across_to = jnp.where(seam_here == 1, BAND - 1 - target, target)
        corner_tiles.append(lookup(column + 2 * col_bit - 1, across_to, inside))
        corner_codes.append(jnp.where(seam_here == 1, 2 * row_bit + 1 - col_bit, 3 - corner_slot).astype(jnp.int32))
    return (edge_tiles, edge_codes, jnp.stack(corner_tiles, axis=1), jnp.stack(corner_codes, axis=1))


def draw_edge_tile(key, part):
    return build_lists(key)[0]


def draw_edge_code(key, part):
    return build_lists(key)[1]


def draw_corner_tile(key, part):
    return build_lists(key)[2]


def draw_corner_code(key, part):
    return build_lists(key)[3]


def draw_vert_diff(key, part):
    folded = jax.random.fold_in(key, 11)
    key_base, key_strong, key_pick, key_depth = jax.random.split(folded, 4)
    base_values = jnp.exp(jax.random.uniform(key_base, (LEVELS, TILES, CELLS), jnp.float32, jnp.log(0.5), jnp.log(20.0)))
    strong_values = jnp.exp(jax.random.uniform(key_strong, (LEVELS, TILES, CELLS), jnp.float32, jnp.log(100.0), jnp.log(2000.0)))
    share = 0.34
    shallowest = LEV_DEV // 2 + 1
    picked = jax.random.uniform(key_pick, (TILES, CELLS), jnp.float32) < share
    mixed_depth = jax.random.randint(key_depth, (TILES, CELLS), shallowest, LEVELS + 1)
    level_index = jnp.arange(LEVELS, dtype=jnp.int32)[:, None, None]
    inside = picked[None] & (level_index < mixed_depth[None])
    return jnp.where(inside, strong_values, base_values).astype(jnp.float32)


def plant(drawn, own_key, low, high):
    spot = [jax.random.randint(jax.random.fold_in(own_key, axis), (), 0, length) for axis, length in enumerate(drawn.shape)]
    main_axis = drawn.shape.index(max(drawn.shape))
    beside = spot[:main_axis] + [(spot[main_axis] + 1) % drawn.shape[main_axis]] + spot[main_axis + 1:]
    return drawn.at[tuple(spot)].set(low).at[tuple(beside)].set(high)


def block_scale(own_key, extent, pieces, least, largest):
    def one(dim, shards_of):
        draws = jax.random.uniform(jax.random.fold_in(jax.random.fold_in(own_key, 6), dim), (shards_of,), jnp.float32, least / len(pieces), largest / len(pieces))
        return jnp.repeat(jnp.exp(draws), extent[dim] // shards_of).reshape((-1,) + (1,) * (len(extent) - dim - 1))

    gain = one(*pieces[0])
    for cut in pieces[1:]:
        gain = gain * one(*cut)
    return gain


def centred(stream_key, shape, deviation, limit, cuts=(), held_as=jnp.bfloat16):
    level = block_scale(stream_key, shape, cuts, -0.22, 0.18) if cuts else 1.0
    result = jax.random.normal(stream_key, shape, jnp.float32) * deviation * level
    return jnp.minimum(jnp.maximum(result, -limit), limit).astype(held_as)


def setup_inputs(seed: int = 0) -> dict:
    seeds = jax.random.split(jax.random.key(seed), 11)
    return {
        "cotangent": centred(seeds[0], (LEVELS, TRACERS, TILES, CELLS), 1.0, 6.0, ((2, 32),), jnp.float32),
        "courant_x": centred(seeds[1], (LEVELS, TILES, CELLS), 0.2, 0.6, ((1, 32),), jnp.float32),
        "courant_y": centred(seeds[2], (LEVELS, TILES, CELLS), 0.2, 0.6, ((1, 32),), jnp.float32),
        "diffusivity": jnp.clip(jnp.exp(math.log(0.16) - 1.3862944 * jax.random.uniform(seeds[3], (TILES, CELLS), jnp.float32) ** block_scale(seeds[3], (TILES, CELLS), ((0, 32),), -0.2, 0.2)), 0.04, 0.16),
        "vert_diff": draw_vert_diff(jax.random.fold_in(seeds[10], 71), 0),
        "level_count": plant(jax.random.randint(seeds[5], (TILES, CELLS), 0, LEVELS + 1), jax.random.fold_in(seeds[5], 1), 0, LEVELS).astype(jnp.int32),
        "edge_tile": draw_edge_tile(jax.random.fold_in(seeds[10], 71), 0),
        "edge_code": draw_edge_code(jax.random.fold_in(seeds[10], 71), 0),
        "corner_tile": draw_corner_tile(jax.random.fold_in(seeds[10], 71), 0),
        "corner_code": draw_corner_code(jax.random.fold_in(seeds[10], 71), 0),
    }


stencil_offsets = [(0, -1), (0, 1), (-1, 0), (1, 0), (-1, -1), (-1, 1), (1, -1), (1, 1)]

def stencil_weights(diffuse, flow_x, flow_y):
    return [diffuse + 0.5 * flow_x, diffuse - 0.5 * flow_x, diffuse + 0.5 * flow_y, diffuse - 0.5 * flow_y, 0.25 * diffuse, 0.25 * diffuse, 0.25 * diffuse, 0.25 * diffuse]

def eliminate(right_side, coupling_up, coupling_down, initial):

    def advance(state, inputs):
        factor, partial_value = state
        source, upper_term, lower_term = inputs
        divisor = 1.0 + upper_term + lower_term + upper_term * factor
        factor_new = -lower_term / divisor
        partial_new = (source + upper_term * partial_value) / divisor
        return ((factor_new, partial_new), (factor_new, partial_new))
    final_state, outputs = lax.scan(advance, initial, (right_side, coupling_up, coupling_down))
    return outputs

def substitute(factors, partials, below_field):

    def backward(state, inputs):
        factor, partial_value = inputs
        column_value = partial_value - factor * state
        return (column_value, column_value)
    final_state, fields = lax.scan(backward, below_field, (factors, partials), reverse=True)
    return fields

def extend(square, edge_tile, edge_code, corner_tile, corner_code):
    strips = jnp.stack([square[:, :, 0, :], square[:, :, -1, :], square[:, :, :, 0], square[:, :, :, -1]], axis=2)
    corner_cells = jnp.stack([square[:, :, 0, 0], square[:, :, 0, -1], square[:, :, -1, 0], square[:, :, -1, -1]], axis=2)
    safe_edge = jnp.maximum(edge_tile, 0)
    fetched = strips[:, safe_edge, edge_code % 4]
    fetched = jnp.where((edge_code >= 4)[None, :, :, None], fetched[..., ::-1], fetched)
    fetched = fetched * (edge_tile >= 0).astype(jnp.float32)[None, :, :, None]
    safe_corner = jnp.maximum(corner_tile, 0)
    corner_values = corner_cells[:, safe_corner, corner_code] * (corner_tile >= 0).astype(jnp.float32)[None]
    padded = jnp.pad(square, ((0, 0), (0, 0), (1, 1), (1, 1)))
    padded = padded.at[:, :, 0, 1:-1].set(fetched[:, :, 0])
    padded = padded.at[:, :, -1, 1:-1].set(fetched[:, :, 1])
    padded = padded.at[:, :, 1:-1, 0].set(fetched[:, :, 2])
    padded = padded.at[:, :, 1:-1, -1].set(fetched[:, :, 3])
    padded = padded.at[:, :, 0, 0].set(corner_values[:, :, 0])
    padded = padded.at[:, :, 0, -1].set(corner_values[:, :, 1])
    padded = padded.at[:, :, -1, 0].set(corner_values[:, :, 2])
    padded = padded.at[:, :, -1, -1].set(corner_values[:, :, 3])
    return padded

def reference(cotangent, courant_x, courant_y, diffusivity, vert_diff, level_count, edge_tile, edge_code, corner_tile, corner_code):
    depth_index = jnp.arange(LEVELS, dtype=jnp.int32)[:, None, None]
    wet_mask = (depth_index < level_count[None]).astype(jnp.float32)
    coupling = jnp.where(depth_index == 0, jnp.float32(0.0), vert_diff * wet_mask)
    lower = jnp.concatenate([coupling[1:], jnp.zeros_like(coupling[:1])], axis=0)
    diffuse = diffusivity.reshape(1, TILES, EDGE, EDGE)
    flow_x = courant_x.reshape(LEVELS, TILES, EDGE, EDGE)
    flow_y = courant_y.reshape(LEVELS, TILES, EDGE, EDGE)
    weights = stencil_weights(diffuse, flow_x, flow_y)

    def forward(field):
        masked = (field * wet_mask).reshape(LEVELS, TILES, EDGE, EDGE)
        padded = extend(masked, edge_tile, edge_code, corner_tile, corner_code)
        combined = (1.0 - 5.0 * diffuse) * masked
        for (shift_row, shift_col), weight in zip(stencil_offsets, weights):
            combined = combined + weight * padded[:, :, 1 + shift_row:1 + shift_row + EDGE, 1 + shift_col:1 + shift_col + EDGE]
        mixed = combined.reshape(LEVELS, TILES, CELLS) * wet_mask
        initial = (jnp.zeros((TILES, CELLS), jnp.float32), jnp.zeros((TILES, CELLS), jnp.float32))
        factors, partials = eliminate(mixed, coupling, lower, initial)
        return substitute(factors, partials, jnp.zeros((TILES, CELLS), jnp.float32))
    primal_out, pullback = jax.vjp(forward, jnp.zeros((LEVELS, TILES, CELLS), jnp.float32))
    per_tracer = jnp.moveaxis(cotangent, 1, 0)
    adjoint = lax.map(lambda tracer_seed: pullback(tracer_seed)[0], per_tracer)
    return jnp.moveaxis(adjoint, 0, 1)
```

```python
import functools

import jax
import jax.numpy as jnp
import numpy as np
from jax import lax
from jax.experimental import pallas as pl
from jax.experimental.pallas import tpu as pltpu
from jax.sharding import PartitionSpec as P

EDGE = 30
BAND = 8


stencil_offsets = [(0, -1), (0, 1), (-1, 0), (1, 0), (-1, -1), (-1, 1), (1, -1), (1, 1)]


def from_behind(value, axis, steps):
    count = lax.axis_size(axis)
    initial, last = (max(0, -steps), min(count, count - steps))
    return lax.ppermute(value, axis, [(source, source + steps) for source in range(initial, last)])


def shifted_2(value, axis, by):
    devices = lax.axis_size(axis)
    return lax.ppermute(value, axis, [(i, (i + by) % devices) for i in range(devices)])


def stencil_weights(diffuse, flow_x, flow_y):
    return [
        diffuse + 0.5 * flow_x,
        diffuse - 0.5 * flow_x,
        diffuse + 0.5 * flow_y,
        diffuse - 0.5 * flow_y,
        0.25 * diffuse,
        0.25 * diffuse,
        0.25 * diffuse,
        0.25 * diffuse,
    ]


def eliminate(right_side, coupling_up, coupling_down, initial):

    def advance(state, inputs):
        factor, partial_value = state
        source, upper_term, lower_term = inputs
        divisor = 1.0 + upper_term + lower_term + upper_term * factor
        factor_new = -lower_term / divisor
        partial_new = (source + upper_term * partial_value) / divisor
        return ((factor_new, partial_new), (factor_new, partial_new))

    final_state, outputs = lax.scan(advance, initial, (right_side, coupling_up, coupling_down))
    return outputs


def substitute(factors, partials, below_field):

    def backward(state, inputs):
        factor, partial_value = inputs
        column_value = partial_value - factor * state
        return (column_value, column_value)

    final_state, fields = lax.scan(backward, below_field, (factors, partials), reverse=True)
    return fields


def cycle_tables():
    padded_edge = EDGE + 2
    cycle_spots = []
    cell_spots = []
    for border in range(4):
        for position in range(EDGE):
            if border == 0:
                cycle_spots.append(position + 1)
                cell_spots.append(position)
            elif border == 1:
                cycle_spots.append((padded_edge - 1) * padded_edge + position + 1)
                cell_spots.append((EDGE - 1) * EDGE + position)
            elif border == 2:
                cycle_spots.append((position + 1) * padded_edge)
                cell_spots.append(position * EDGE)
            else:
                cycle_spots.append((position + 1) * padded_edge + padded_edge - 1)
                cell_spots.append(position * EDGE + EDGE - 1)
    cycle_spots += [
        0,
        padded_edge - 1,
        (padded_edge - 1) * padded_edge,
        padded_edge * padded_edge - 1,
    ]
    cell_spots += [0, EDGE - 1, (EDGE - 1) * EDGE, EDGE * EDGE - 1]
    placing = np.zeros((len(cycle_spots), EDGE * EDGE), np.float32)
    placing[np.arange(len(cycle_spots)), np.array(cell_spots)] = 1.0
    return (np.array(cycle_spots, np.int32), placing)


def embed(field):
    leading = field.shape[:-1]
    square = field.reshape(leading + (EDGE, EDGE))
    padded = jnp.pad(square, [(0, 0)] * len(leading) + [(1, 1), (1, 1)])
    return padded.reshape(leading + ((EDGE + 2) * (EDGE + 2),))


def shards(
    cotangent,
    courant_x,
    courant_y,
    diffusivity,
    vert_diff,
    level_count,
    edge_tile,
    edge_code,
    corner_tile,
    corner_code,
):
    levels_here = cotangent.shape[0]
    tracers = cotangent.shape[1]
    tiles_here = cotangent.shape[2]
    cells = cotangent.shape[3]
    padded_edge = EDGE + 2
    cycle_size = 4 * EDGE + 4
    lev_count = lax.axis_size("lev")
    depth_index = (
        lax.axis_index("lev") * levels_here
        + jnp.arange(levels_here, dtype=jnp.int32)[:, None, None]
    )
    wet_mask = (depth_index < level_count[None]).astype(jnp.float32)
    coupling = jnp.where(depth_index == 0, jnp.float32(0.0), vert_diff * wet_mask)
    deeper = from_behind(coupling[0], "lev", -1)
    coupling_down = jnp.concatenate([coupling[1:], deeper[None]], axis=0)[:, None]
    coupling_up = coupling[:, None]
    initial = (
        jnp.zeros((1, tiles_here, cells), jnp.float32),
        jnp.zeros((tracers, tiles_here, cells), jnp.float32),
    )
    for sweep_index in range(lev_count - 1):
        factors, partials = eliminate(cotangent, coupling_up, coupling_down, initial)
        initial = from_behind((factors[-1], partials[-1]), "lev", 1)
    factors, partials = eliminate(cotangent, coupling_up, coupling_down, initial)
    below_field = jnp.zeros((tracers, tiles_here, cells), jnp.float32)
    for sweep_index in range(lev_count - 1):
        fields = substitute(factors, partials, below_field)
        below_field = from_behind(fields[0], "lev", -1)
    solved = substitute(factors, partials, below_field)
    weighted = solved * wet_mask[:, None]
    weighted_ext = embed(weighted)
    diffuse_ext = embed(diffusivity)[None, None]
    flow_x_ext = embed(courant_x)[:, None]
    flow_y_ext = embed(courant_y)[:, None]
    weights = stencil_weights(diffuse_ext, flow_x_ext, flow_y_ext)
    leading = weighted_ext.shape[:-1]
    spread = jnp.zeros_like(weighted_ext)
    for (shift_row, shift_col), weight in zip(stencil_offsets, weights):
        contribution = weight * weighted_ext
        offset = shift_row * padded_edge + shift_col
        if offset > 0:
            shifted = jnp.concatenate(
                [jnp.zeros(leading + (offset,), jnp.float32), contribution[..., :-offset]], axis=-1
            )
        else:
            shifted = jnp.concatenate(
                [contribution[..., -offset:], jnp.zeros(leading + (-offset,), jnp.float32)], axis=-1
            )
        spread = spread + shifted
    cycle_spots, placing = cycle_tables()
    outgoing = jnp.take(spread, jnp.asarray(cycle_spots), axis=3)
    interior = spread.reshape(leading + (padded_edge, padded_edge))[..., 1:-1, 1:-1].reshape(
        solved.shape
    )
    partners = jnp.concatenate([edge_tile, corner_tile], axis=1)

    def collect(gathered_sum, portion, first_tile):
        tile_span = portion.shape[2]
        onehot = (
            partners[:, :, None]
            == first_tile + jnp.arange(tile_span, dtype=jnp.int32)[None, None, :]
        ).astype(jnp.float32)
        return gathered_sum + jnp.einsum(
            "tkw,dnwr->dntkr", onehot, portion, precision=lax.Precision.HIGHEST
        )

    tile_count = lax.axis_size("tile")
    own_index = lax.axis_index("tile")
    reach = (2 * BAND + tiles_here - 1) // tiles_here
    fetched = collect(
        jnp.zeros((levels_here, tracers, tiles_here, 8, cycle_size), jnp.float32),
        outgoing,
        own_index * tiles_here,
    )
    for distance in range(-reach, reach + 1):
        if distance != 0:
            portion = shifted_2(outgoing, "tile", distance)
            source = (own_index - distance) % tile_count
            fetched = collect(fetched, portion, source * tiles_here)
    side_values = fetched[:, :, :, :4, : 4 * EDGE].reshape(
        levels_here, tracers, tiles_here, 4, 4, EDGE
    )
    side_choice = (
        (edge_code % 4)[:, :, None] == jnp.arange(4, dtype=jnp.int32)[None, None, :]
    ).astype(jnp.float32)
    strips = jnp.sum(side_values * side_choice[None, None, :, :, :, None], axis=4)
    strips = jnp.where((edge_code >= 4)[None, None, :, :, None], strips[..., ::-1], strips)
    corner_values = fetched[:, :, :, 4:, 4 * EDGE :]
    corner_choice = (
        corner_code[:, :, None] == jnp.arange(4, dtype=jnp.int32)[None, None, :]
    ).astype(jnp.float32)
    corner_picked = jnp.sum(corner_values * corner_choice[None, None], axis=4)
    arriving = jnp.concatenate(
        [strips.reshape(levels_here, tracers, tiles_here, 4 * EDGE), corner_picked], axis=3
    )
    returned = jnp.einsum(
        "dntr,rc->dntc", arriving, jnp.asarray(placing), precision=lax.Precision.HIGHEST
    )
    diffuse_here = diffusivity[None, None]
    return wet_mask[:, None] * ((1.0 - 5.0 * diffuse_here) * weighted + interior + returned)


PADDED = 1024
SIDE_LANES = 32
MESH = pl.DeviceIdType.MESH


def strip_selector():
    chosen = np.zeros((PADDED + 128, 256), np.float32)
    for j in range(EDGE):
        for side, lane in enumerate([PADDED - EDGE + j, EDGE * EDGE + j, EDGE * j, EDGE * j + EDGE - 1]):
            chosen[lane, SIDE_LANES * side + j] = 1.0
            chosen[lane, 128 + SIDE_LANES * side + EDGE - 1 - j] = 1.0
    for corner, cell in enumerate([0, EDGE - 1, (EDGE - 1) * EDGE, EDGE * EDGE - 1]):
        chosen[PADDED + cell % 128, SIDE_LANES * corner + EDGE] = 1.0
    return jnp.asarray(chosen, jnp.bfloat16)


def strip_placer():
    placing = np.zeros((128, PADDED), np.float32)
    for j in range(EDGE):
        for side, cell in enumerate([j, (EDGE - 1) * EDGE + j, EDGE * j, EDGE * j + EDGE - 1]):
            placing[SIDE_LANES * side + j, cell] = 1.0
    for corner, cell in enumerate([0, EDGE - 1, (EDGE - 1) * EDGE, EDGE * EDGE - 1]):
        placing[SIDE_LANES * corner + EDGE, cell] = 1.0
    return jnp.asarray(placing, jnp.bfloat16)


def split_dot(left, right):
    high = left.astype(jnp.bfloat16)
    low = (left - high.astype(jnp.float32)).astype(jnp.bfloat16)
    return jnp.dot(high, right, preferred_element_type=jnp.float32) + jnp.dot(
        low, right, preferred_element_type=jnp.float32
    )


def four_times(pair):
    return jnp.concatenate([pair, pair, pair, pair], axis=0)


def widen(rows):
    return jnp.concatenate(
        [rows, jnp.zeros((rows.shape[0], PADDED - rows.shape[1]), rows.dtype)], axis=1
    )


def solve_kernel(
    code_ref, cot_ref, cx_ref, cy_ref, dif_ref, vd_ref, lc_ref, sel_ref,
    base_ref, strips_ref, factor_ref, partial_ref, edge_ref,
):
    levels = cot_ref.shape[0]
    cells = cot_ref.shape[3]
    depth = four_times(lc_ref[...])

    def coupling(k):
        if k == 0 or k == levels:
            return jnp.zeros((8, cells), jnp.float32)
        return jnp.where(k < depth, four_times(vd_ref[k]), 0.0)

    factor = jnp.zeros((8, cells), jnp.float32)
    partial_value = jnp.zeros((8, cells), jnp.float32)
    upper = coupling(0)
    for k in range(levels):
        lower = coupling(k + 1)
        source = jnp.concatenate([cot_ref[k, n] for n in range(4)], axis=0)
        inverse = 1.0 / ((1.0 + upper + lower) + upper * factor)
        factor = -lower * inverse
        partial_value = (source + upper * partial_value) * inverse
        factor_ref[k] = factor
        partial_ref[k] = partial_value
        upper = lower

    lane = lax.broadcasted_iota(jnp.int32, (8, PADDED), 1)
    row_lane = jnp.where(lane >= PADDED - EDGE, lane - (PADDED - EDGE), lane)
    column = lax.rem(row_lane, EDGE)
    first = column == 0
    last = column == EDGE - 1
    inside = lane < cells
    short = lax.broadcasted_iota(jnp.int32, (8, 128), 1)
    corner_0 = (short == 0) | (short == EDGE - 1)
    corner_6 = short == ((EDGE - 1) * EDGE) % 128
    corner_7 = short == (EDGE * EDGE - 1) % 128
    diffuse = widen(four_times(dif_ref[...]))
    quarter = 0.25 * diffuse
    centre = 1.0 - 5.0 * diffuse
    wide_depth = widen(depth)
    solved = jnp.zeros((8, cells), jnp.float32)
    for k in reversed(range(levels)):
        solved = partial_ref[k] - factor_ref[k] * solved
        u = widen(jnp.where(k < depth, solved, 0.0))
        half_x = 0.5 * widen(four_times(cx_ref[k]))
        half_y = 0.5 * widen(four_times(cy_ref[k]))
        diagonal = quarter * u
        both = pltpu.roll(diagonal, EDGE, 1) + pltpu.roll(diagonal, PADDED - EDGE, 1)
        west = both + (diffuse + half_x) * u
        east = both + (diffuse - half_x) * u
        spread = pltpu.roll((diffuse + half_y) * u, PADDED - EDGE, 1)
        spread = spread + pltpu.roll((diffuse - half_y) * u, EDGE, 1)
        spread = spread + pltpu.roll(jnp.where(first, 0.0, west), PADDED - 1, 1)
        spread = spread + pltpu.roll(jnp.where(last, 0.0, east), 1, 1)
        base_ref[k] = jnp.where(k < wide_depth, centre * u + spread, 0.0)
        edge_ref[8 * k : 8 * k + 8, :PADDED] = jnp.where(
            inside, jnp.where(first, west, east), spread
        )
        edge_ref[8 * k : 8 * k + 8, PADDED:] = (
            jnp.where(corner_0, diagonal[:, 0:128], 0.0)
            + jnp.where(corner_6, diagonal[:, 768:896], 0.0)
            + jnp.where(corner_7, diagonal[:, 896:1024], 0.0)
        )
    both_ways = split_dot(edge_ref[...], sel_ref[...])
    parity = lax.rem(lax.broadcasted_iota(jnp.int32, (8, 128), 0), 2)
    code = jnp.zeros((8, 128), jnp.int32)
    for i in range(2):
        for side in range(4):
            code = jnp.where((parity == i) & (short // SIDE_LANES == side), code_ref[i, side], code)
    flipped = (code >= 4) & (lax.rem(short, SIDE_LANES) < EDGE)
    for k in range(levels):
        rows = both_ways[8 * k : 8 * k + 8]
        strips_ref[k] = jnp.where(flipped, rows[:, 128:], rows[:, :128])


def send_kernel(count, reach, strips_ref, near_ref, own_sem, send_sem, recv_sem):
    me = lax.axis_index("tile")
    barrier = pltpu.get_barrier_semaphore()
    offsets = [o for o in range(-reach, reach + 1) if o != 0]
    for o in offsets:
        pl.semaphore_signal(
            barrier, inc=1, device_id={"tile": lax.rem(me + o + count, count)}, device_id_type=MESH
        )
    own = pltpu.make_async_copy(strips_ref, near_ref.at[reach], own_sem)
    own.start()
    pl.semaphore_wait(barrier, len(offsets))
    copies = []
    for o in offsets:
        copy = pltpu.make_async_remote_copy(
            src_ref=strips_ref,
            dst_ref=near_ref.at[reach - o],
            send_sem=send_sem.at[reach + o],
            recv_sem=recv_sem.at[reach - o],
            device_id={"tile": lax.rem(me + o + count, count)},
            device_id_type=MESH,
        )
        copy.start()
        copies.append(copy)
    own.wait()
    for copy in copies:
        copy.wait()


def place_kernel(
    count, reach, et_ref, ec_ref, ct_ref, cc_ref, near_ref, base_ref, lc_ref, place_ref,
    out_ref, arriving_ref,
):
    levels = base_ref.shape[0]
    cells = out_ref.shape[3]
    me = lax.axis_index("tile")
    lane = lax.broadcasted_iota(jnp.int32, (8, 128), 1)
    parity = lax.rem(lax.broadcasted_iota(jnp.int32, (8, 128), 0), 2)
    group = lane // SIDE_LANES
    spot = lax.rem(lane, SIDE_LANES)
    total = jnp.zeros((levels, 8, 128), jnp.float32)
    for i in range(2):
        for tiles_ref, codes_ref, wanted in (
            (et_ref, ec_ref, spot < EDGE),
            (ct_ref, cc_ref, spot == EDGE),
        ):
            for side in range(4):
                tile = tiles_ref[i, side]
                there = jnp.maximum(tile, 0)
                slot = lax.rem(there // 2 - me + reach + count, count)
                slot = jnp.where(tile < 0, 0, slot)
                values = near_ref[slot]
                values = jnp.where(
                    lax.rem(there, 2) == i, values, pltpu.roll(values, 1 if i == 1 else 7, 1)
                )
                shift = lax.rem(SIDE_LANES * (side - lax.rem(codes_ref[i, side], 4)) + 128, 128)
                values = pltpu.roll(values, shift, 2)
                chosen = wanted & (group == side) & (parity == i) & (tile >= 0)
                total = jnp.where(chosen[None], values, total)
    for k in range(levels):
        arriving_ref[8 * k : 8 * k + 8] = total[k]
    returned = split_dot(arriving_ref[...], place_ref[...])
    depth = four_times(lc_ref[...])
    for k in range(levels):
        result = base_ref[k][:, :cells] + jnp.where(
            k < depth, returned[8 * k : 8 * k + 8, :cells], 0.0
        )
        for n in range(4):
            out_ref[k, n] = result[2 * n : 2 * n + 2]


def shards_fast(
    cotangent,
    courant_x,
    courant_y,
    diffusivity,
    vert_diff,
    level_count,
    edge_tile,
    edge_code,
    corner_tile,
    corner_code,
):
    levels, tracers, tiles_here, cells = cotangent.shape
    count = lax.axis_size("tile")
    reach = (2 * BAND + tiles_here - 1) // tiles_here
    vmem = pl.BlockSpec(memory_space=pltpu.VMEM)
    smem = pl.BlockSpec(memory_space=pltpu.SMEM)
    anywhere = pl.BlockSpec(memory_space=pl.ANY)
    base, strips = pl.pallas_call(
        solve_kernel,
        name="solve",
        out_shape=(
            jax.ShapeDtypeStruct((levels, 8, PADDED), jnp.float32),
            jax.ShapeDtypeStruct((levels, 8, 128), jnp.float32),
        ),
        in_specs=[smem] + [vmem] * 7,
        out_specs=(vmem, vmem),
        scratch_shapes=[
            pltpu.VMEM((levels, 8, cells), jnp.float32),
            pltpu.VMEM((levels, 8, cells), jnp.float32),
            pltpu.VMEM((8 * levels, PADDED + 128), jnp.float32),
        ],
        compiler_params=pltpu.CompilerParams(vmem_limit_bytes=40 << 20),
    )(edge_code, cotangent, courant_x, courant_y, diffusivity, vert_diff, level_count, strip_selector())
    near = pl.pallas_call(
        functools.partial(send_kernel, count, reach),
        name="send",
        out_shape=jax.ShapeDtypeStruct((2 * reach + 1, levels, 8, 128), jnp.float32),
        in_specs=[anywhere],
        out_specs=anywhere,
        scratch_shapes=[
            pltpu.SemaphoreType.DMA,
            pltpu.SemaphoreType.DMA((2 * reach + 1,)),
            pltpu.SemaphoreType.DMA((2 * reach + 1,)),
        ],
        compiler_params=pltpu.CompilerParams(collective_id=0, has_side_effects=True),
    )(strips)
    return pl.pallas_call(
        functools.partial(place_kernel, count, reach),
        name="place",
        out_shape=jax.ShapeDtypeStruct(cotangent.shape, jnp.float32),
        in_specs=[smem] * 4 + [vmem] * 4,
        out_specs=vmem,
        scratch_shapes=[pltpu.VMEM((8 * levels, 128), jnp.float32)],
        compiler_params=pltpu.CompilerParams(vmem_limit_bytes=40 << 20),
    )(edge_tile, edge_code, corner_tile, corner_code, near, base, level_count, strip_placer())


def solution(mesh):
    placed = (
        P("lev", None, "tile", None),
        P("lev", "tile", None),
        P("lev", "tile", None),
        P("tile", None),
        P("lev", "tile", None),
        P("tile", None),
        P("tile", None),
        P("tile", None),
        P("tile", None),
        P("tile", None),
    )
    fast = mesh.shape["lev"] == 1 and mesh.shape["tile"] > 2 * BAND
    return jax.shard_map(
        shards_fast if fast else shards, mesh=mesh, in_specs=placed, out_specs=P("lev", None, "tile", None), check_vma=False
    )
```

```python
import functools

import jax
import jax.numpy as jnp
import numpy as np
from jax import lax
from jax.experimental import pallas as pl
from jax.experimental.pallas import tpu as pltpu
from jax.sharding import PartitionSpec as P

EDGE = 30
BAND = 8


stencil_offsets = [(0, -1), (0, 1), (-1, 0), (1, 0), (-1, -1), (-1, 1), (1, -1), (1, 1)]


def from_behind(value, axis, steps):
    count = lax.axis_size(axis)
    initial, last = (max(0, -steps), min(count, count - steps))
    return lax.ppermute(value, axis, [(source, source + steps) for source in range(initial, last)])


def shifted_2(value, axis, by):
    devices = lax.axis_size(axis)
    return lax.ppermute(value, axis, [(i, (i + by) % devices) for i in range(devices)])


def stencil_weights(diffuse, flow_x, flow_y):
    return [
        diffuse + 0.5 * flow_x,
        diffuse - 0.5 * flow_x,
        diffuse + 0.5 * flow_y,
        diffuse - 0.5 * flow_y,
        0.25 * diffuse,
        0.25 * diffuse,
        0.25 * diffuse,
        0.25 * diffuse,
    ]


def eliminate(right_side, coupling_up, coupling_down, initial):

    def advance(state, inputs):
        factor, partial_value = state
        source, upper_term, lower_term = inputs
        divisor = 1.0 + upper_term + lower_term + upper_term * factor
        factor_new = -lower_term / divisor
        partial_new = (source + upper_term * partial_value) / divisor
        return ((factor_new, partial_new), (factor_new, partial_new))

    final_state, outputs = lax.scan(advance, initial, (right_side, coupling_up, coupling_down))
    return outputs


def substitute(factors, partials, below_field):

    def backward(state, inputs):
        factor, partial_value = inputs
        column_value = partial_value - factor * state
        return (column_value, column_value)

    final_state, fields = lax.scan(backward, below_field, (factors, partials), reverse=True)
    return fields


def cycle_tables():
    padded_edge = EDGE + 2
    cycle_spots = []
    cell_spots = []
    for border in range(4):
        for position in range(EDGE):
            if border == 0:
                cycle_spots.append(position + 1)
                cell_spots.append(position)
            elif border == 1:
                cycle_spots.append((padded_edge - 1) * padded_edge + position + 1)
                cell_spots.append((EDGE - 1) * EDGE + position)
            elif border == 2:
                cycle_spots.append((position + 1) * padded_edge)
                cell_spots.append(position * EDGE)
            else:
                cycle_spots.append((position + 1) * padded_edge + padded_edge - 1)
                cell_spots.append(position * EDGE + EDGE - 1)
    cycle_spots += [
        0,
        padded_edge - 1,
        (padded_edge - 1) * padded_edge,
        padded_edge * padded_edge - 1,
    ]
    cell_spots += [0, EDGE - 1, (EDGE - 1) * EDGE, EDGE * EDGE - 1]
    placing = np.zeros((len(cycle_spots), EDGE * EDGE), np.float32)
    placing[np.arange(len(cycle_spots)), np.array(cell_spots)] = 1.0
    return (np.array(cycle_spots, np.int32), placing)


def embed(field):
    leading = field.shape[:-1]
    square = field.reshape(leading + (EDGE, EDGE))
    padded = jnp.pad(square, [(0, 0)] * len(leading) + [(1, 1), (1, 1)])
    return padded.reshape(leading + ((EDGE + 2) * (EDGE + 2),))


def shards(
    cotangent,
    courant_x,
    courant_y,
    diffusivity,
    vert_diff,
    level_count,
    edge_tile,
    edge_code,
    corner_tile,
    corner_code,
):
    levels_here = cotangent.shape[0]
    tracers = cotangent.shape[1]
    tiles_here = cotangent.shape[2]
    cells = cotangent.shape[3]
    padded_edge = EDGE + 2
    cycle_size = 4 * EDGE + 4
    lev_count = lax.axis_size("lev")
    depth_index = (
        lax.axis_index("lev") * levels_here
        + jnp.arange(levels_here, dtype=jnp.int32)[:, None, None]
    )
    wet_mask = (depth_index < level_count[None]).astype(jnp.float32)
    coupling = jnp.where(depth_index == 0, jnp.float32(0.0), vert_diff * wet_mask)
    deeper = from_behind(coupling[0], "lev", -1)
    coupling_down = jnp.concatenate([coupling[1:], deeper[None]], axis=0)[:, None]
    coupling_up = coupling[:, None]
    initial = (
        jnp.zeros((1, tiles_here, cells), jnp.float32),
        jnp.zeros((tracers, tiles_here, cells), jnp.float32),
    )
    for sweep_index in range(lev_count - 1):
        factors, partials = eliminate(cotangent, coupling_up, coupling_down, initial)
        initial = from_behind((factors[-1], partials[-1]), "lev", 1)
    factors, partials = eliminate(cotangent, coupling_up, coupling_down, initial)
    below_field = jnp.zeros((tracers, tiles_here, cells), jnp.float32)
    for sweep_index in range(lev_count - 1):
        fields = substitute(factors, partials, below_field)
        below_field = from_behind(fields[0], "lev", -1)
    solved = substitute(factors, partials, below_field)
    weighted = solved * wet_mask[:, None]
    weighted_ext = embed(weighted)
    diffuse_ext = embed(diffusivity)[None, None]
    flow_x_ext = embed(courant_x)[:, None]
    flow_y_ext = embed(courant_y)[:, None]
    weights = stencil_weights(diffuse_ext, flow_x_ext, flow_y_ext)
    leading = weighted_ext.shape[:-1]
    spread = jnp.zeros_like(weighted_ext)
    for (shift_row, shift_col), weight in zip(stencil_offsets, weights):
        contribution = weight * weighted_ext
        offset = shift_row * padded_edge + shift_col
        if offset > 0:
            shifted = jnp.concatenate(
                [jnp.zeros(leading + (offset,), jnp.float32), contribution[..., :-offset]], axis=-1
            )
        else:
            shifted = jnp.concatenate(
                [contribution[..., -offset:], jnp.zeros(leading + (-offset,), jnp.float32)], axis=-1
            )
        spread = spread + shifted
    cycle_spots, placing = cycle_tables()
    outgoing = jnp.take(spread, jnp.asarray(cycle_spots), axis=3)
    interior = spread.reshape(leading + (padded_edge, padded_edge))[..., 1:-1, 1:-1].reshape(
        solved.shape
    )
    partners = jnp.concatenate([edge_tile, corner_tile], axis=1)

    def collect(gathered_sum, portion, first_tile):
        tile_span = portion.shape[2]
        onehot = (
            partners[:, :, None]
            == first_tile + jnp.arange(tile_span, dtype=jnp.int32)[None, None, :]
        ).astype(jnp.float32)
        return gathered_sum + jnp.einsum(
            "tkw,dnwr->dntkr", onehot, portion, precision=lax.Precision.HIGHEST
        )

    tile_count = lax.axis_size("tile")
    own_index = lax.axis_index("tile")
    reach = (2 * BAND + tiles_here - 1) // tiles_here
    fetched = collect(
        jnp.zeros((levels_here, tracers, tiles_here, 8, cycle_size), jnp.float32),
        outgoing,
        own_index * tiles_here,
    )
    for distance in range(-reach, reach + 1):
        if distance != 0:
            portion = shifted_2(outgoing, "tile", distance)
            source = (own_index - distance) % tile_count
            fetched = collect(fetched, portion, source * tiles_here)
    side_values = fetched[:, :, :, :4, : 4 * EDGE].reshape(
        levels_here, tracers, tiles_here, 4, 4, EDGE
    )
    side_choice = (
        (edge_code % 4)[:, :, None] == jnp.arange(4, dtype=jnp.int32)[None, None, :]
    ).astype(jnp.float32)
    strips = jnp.sum(side_values * side_choice[None, None, :, :, :, None], axis=4)
    strips = jnp.where((edge_code >= 4)[None, None, :, :, None], strips[..., ::-1], strips)
    corner_values = fetched[:, :, :, 4:, 4 * EDGE :]
    corner_choice = (
        corner_code[:, :, None] == jnp.arange(4, dtype=jnp.int32)[None, None, :]
    ).astype(jnp.float32)
    corner_picked = jnp.sum(corner_values * corner_choice[None, None], axis=4)
    arriving = jnp.concatenate(
        [strips.reshape(levels_here, tracers, tiles_here, 4 * EDGE), corner_picked], axis=3
    )
    returned = jnp.einsum(
        "dntr,rc->dntc", arriving, jnp.asarray(placing), precision=lax.Precision.HIGHEST
    )
    diffuse_here = diffusivity[None, None]
    return wet_mask[:, None] * ((1.0 - 5.0 * diffuse_here) * weighted + interior + returned)


PADDED = 1024
SIDE_LANES = 32
PLANE = 4
MESH = pl.DeviceIdType.MESH


def strip_selector():
    chosen = np.zeros((PADDED + 128, 256), np.float32)
    for j in range(EDGE):
        for side, lane in enumerate([PADDED - EDGE + j, EDGE * EDGE + j, EDGE * j, EDGE * j + EDGE - 1]):
            chosen[lane, SIDE_LANES * side + j] = 1.0
            chosen[lane, 128 + SIDE_LANES * side + EDGE - 1 - j] = 1.0
    for corner, cell in enumerate([0, EDGE - 1, (EDGE - 1) * EDGE, EDGE * EDGE - 1]):
        chosen[PADDED + cell % 128, SIDE_LANES * corner + EDGE] = 1.0
    return jnp.asarray(chosen, jnp.bfloat16)


def strip_placer():
    placing = np.zeros((128, PADDED), np.float32)
    for j in range(EDGE):
        for side, cell in enumerate([j, (EDGE - 1) * EDGE + j, EDGE * j, EDGE * j + EDGE - 1]):
            placing[SIDE_LANES * side + j, cell] = 1.0
    for corner, cell in enumerate([0, EDGE - 1, (EDGE - 1) * EDGE, EDGE * EDGE - 1]):
        placing[SIDE_LANES * corner + EDGE, cell] = 1.0
    return jnp.asarray(placing, jnp.bfloat16)


def split_dot(left, right):
    high = left.astype(jnp.bfloat16)
    low = (left - high.astype(jnp.float32)).astype(jnp.bfloat16)
    return jnp.dot(high, right, preferred_element_type=jnp.float32) + jnp.dot(
        low, right, preferred_element_type=jnp.float32
    )


def four_times(pair):
    return jnp.concatenate([pair, pair, pair, pair], axis=0)


def widen(rows):
    return jnp.concatenate(
        [rows, jnp.zeros((rows.shape[0], PADDED - rows.shape[1]), rows.dtype)], axis=1
    )


def solve_kernel(
    code_hbm, cot_hbm, cx_hbm, cy_hbm, dif_hbm, vd_hbm, lc_hbm, sel_hbm,
    base_ref, strips_ref, factor_ref, partial_ref, edge_ref,
    code_ref, cot_ref, cx_ref, cy_ref, dif_ref, vd_ref, lc_ref, sel_ref, sems,
):
    levels = cot_ref.shape[0]
    cells = cot_ref.shape[3]
    pairs = [
        (lc_hbm, lc_ref),
        (vd_hbm, vd_ref),
        (cot_hbm, cot_ref),
        (dif_hbm, dif_ref),
        (cx_hbm, cx_ref),
        (cy_hbm, cy_ref),
        (code_hbm, code_ref),
        (sel_hbm, sel_ref),
    ]
    copies = [
        pltpu.make_async_copy(source, target, sems.at[i])
        for i, (source, target) in enumerate(pairs)
    ]
    for copy in copies:
        copy.start()
    for copy in copies[:3]:
        copy.wait()
    depth = four_times(lc_ref[...])

    def coupling(k):
        if k == 0 or k == levels:
            return jnp.zeros((8, cells), jnp.float32)
        return jnp.where(k < depth, four_times(vd_ref[k]), 0.0)

    factor = jnp.zeros((8, cells), jnp.float32)
    partial_value = jnp.zeros((8, cells), jnp.float32)
    upper = coupling(0)
    for k in range(levels):
        lower = coupling(k + 1)
        source = jnp.concatenate([cot_ref[k, n] for n in range(4)], axis=0)
        inverse = 1.0 / ((1.0 + upper + lower) + upper * factor)
        factor = -lower * inverse
        partial_value = (source + upper * partial_value) * inverse
        factor_ref[k] = factor
        partial_ref[k] = partial_value
        upper = lower

    lane = lax.broadcasted_iota(jnp.int32, (8, PADDED), 1)
    row_lane = jnp.where(lane >= PADDED - EDGE, lane - (PADDED - EDGE), lane)
    column = lax.rem(row_lane, EDGE)
    first = column == 0
    last = column == EDGE - 1
    inside = lane < cells
    short = lax.broadcasted_iota(jnp.int32, (8, 128), 1)
    corner_0 = (short == 0) | (short == EDGE - 1)
    corner_6 = short == ((EDGE - 1) * EDGE) % 128
    corner_7 = short == (EDGE * EDGE - 1) % 128
    for copy in copies[3:6]:
        copy.wait()
    diffuse = widen(four_times(dif_ref[...]))
    quarter = 0.25 * diffuse
    centre = 1.0 - 5.0 * diffuse
    wide_depth = widen(depth)
    solved = jnp.zeros((8, cells), jnp.float32)
    for k in reversed(range(levels)):
        solved = partial_ref[k] - factor_ref[k] * solved
        u = widen(jnp.where(k < depth, solved, 0.0))
        half_x = 0.5 * widen(four_times(cx_ref[k]))
        half_y = 0.5 * widen(four_times(cy_ref[k]))
        diagonal = quarter * u
        both = pltpu.roll(diagonal, EDGE, 1) + pltpu.roll(diagonal, PADDED - EDGE, 1)
        west = both + (diffuse + half_x) * u
        east = both + (diffuse - half_x) * u
        spread = pltpu.roll((diffuse + half_y) * u, PADDED - EDGE, 1)
        spread = spread + pltpu.roll((diffuse - half_y) * u, EDGE, 1)
        spread = spread + pltpu.roll(jnp.where(first, 0.0, west), PADDED - 1, 1)
        spread = spread + pltpu.roll(jnp.where(last, 0.0, east), 1, 1)
        base_ref[k] = jnp.where(k < wide_depth, centre * u + spread, 0.0)
        edge_ref[8 * k : 8 * k + 8, :PADDED] = jnp.where(
            inside, jnp.where(first, west, east), spread
        )
        edge_ref[8 * k : 8 * k + 8, PADDED:] = (
            jnp.where(corner_0, diagonal[:, 0:128], 0.0)
            + jnp.where(corner_6, diagonal[:, 768:896], 0.0)
            + jnp.where(corner_7, diagonal[:, 896:1024], 0.0)
        )
    for copy in copies[6:]:
        copy.wait()
    both_ways = split_dot(edge_ref[...], sel_ref[...])
    parity = lax.rem(lax.broadcasted_iota(jnp.int32, (8, 128), 0), 2)
    code = jnp.zeros((8, 128), jnp.int32)
    for i in range(2):
        for side in range(4):
            code = jnp.where((parity == i) & (short // SIDE_LANES == side), code_ref[i, side], code)
    flipped = (code >= 4) & (lax.rem(short, SIDE_LANES) < EDGE)
    for k in range(levels):
        rows = both_ways[8 * k : 8 * k + 8]
        strips_ref[k] = jnp.where(flipped, rows[:, 128:], rows[:, :128])


def send_kernel(count, strips_ref, near_ref, own_sem, send_sem, recv_sem):
    chips = count // 2
    me = lax.axis_index("tile")
    chip = me // 2
    core = lax.rem(me, 2)
    place = lax.rem(chip, PLANE)

    def at(steps):
        return 2 * lax.rem(chip + steps + chips, chips) + core

    partner = me + 1 - 2 * core
    wraps = [(place + j) // PLANE for j in range(PLANE)]
    beside = [at(j - PLANE * wraps[j]) for j in range(PLANE)]
    above, below = at(PLANE), at(-PLANE)
    barrier = pltpu.get_barrier_semaphore()
    peers = [partner, above, below] + beside[1:]
    for peer in peers:
        pl.semaphore_signal(barrier, inc=1, device_id={"tile": peer}, device_id_type=MESH)
    own = pltpu.make_async_copy(strips_ref, near_ref.at[PLANE, core], own_sem)
    own.start()
    pl.semaphore_wait(barrier, len(peers))
    copies = []

    def send(source, spot, to):
        copy = pltpu.make_async_remote_copy(
            src_ref=source,
            dst_ref=near_ref.at[spot, core],
            send_sem=send_sem.at[len(copies)],
            recv_sem=recv_sem.at[spot, core],
            device_id={"tile": to},
            device_id_type=MESH,
        )
        copy.start()
        copies.append(copy)

    def arrived(spot, side):
        pltpu.make_async_remote_copy(
            src_ref=strips_ref,
            dst_ref=near_ref.at[spot, side],
            send_sem=own_sem,
            recv_sem=recv_sem.at[spot, side],
            device_id={"tile": partner},
            device_id_type=MESH,
        ).wait_recv()

    def share(spot):
        send(near_ref.at[spot, core], spot, partner)

    send(strips_ref, 0, above)
    send(strips_ref, 2 * PLANE, below)
    for j in range(1, PLANE):
        send(strips_ref, PLANE - j + PLANE * wraps[j], beside[j])
    send(strips_ref, PLANE, partner)
    arrived(0, core)
    arrived(2 * PLANE, core)
    for j in range(1, PLANE):
        source = near_ref.at[2 * PLANE - 2 * PLANE * wraps[j], core]
        send(source, 2 * PLANE - PLANE * wraps[j] - j, beside[j])
    share(0)
    share(2 * PLANE)
    for j in range(1, PLANE):
        spot = PLANE + j - PLANE * wraps[j]
        arrived(spot, core)
        share(spot)
    for j in range(1, PLANE):
        spot = j + PLANE * wraps[j]
        arrived(spot, core)
        share(spot)
    for spot in range(2 * PLANE + 1):
        arrived(spot, 1 - core)
    own.wait()
    for copy in copies:
        copy.wait_send()


def place_kernel(
    count, et_ref, ec_ref, ct_ref, cc_ref, near_ref, base_ref, lc_ref, place_ref,
    out_ref, arriving_ref,
):
    levels = base_ref.shape[0]
    cells = out_ref.shape[3]
    me = lax.axis_index("tile")
    lane = lax.broadcasted_iota(jnp.int32, (8, 128), 1)
    parity = lax.rem(lax.broadcasted_iota(jnp.int32, (8, 128), 0), 2)
    group = lane // SIDE_LANES
    spot = lax.rem(lane, SIDE_LANES)
    total = jnp.zeros((levels, 8, 128), jnp.float32)
    for i in range(2):
        for tiles_ref, codes_ref, wanted in (
            (et_ref, ec_ref, spot < EDGE),
            (ct_ref, cc_ref, spot == EDGE),
        ):
            for side in range(4):
                tile = tiles_ref[i, side]
                there = jnp.maximum(tile, 0)
                slot = lax.rem(there // 4 - me // 2 + PLANE + count // 2, count // 2)
                slot = jnp.where(tile < 0, 0, slot)
                values = near_ref[slot, lax.rem(there // 2, 2)]
                values = jnp.where(
                    lax.rem(there, 2) == i, values, pltpu.roll(values, 1 if i == 1 else 7, 1)
                )
                shift = lax.rem(SIDE_LANES * (side - lax.rem(codes_ref[i, side], 4)) + 128, 128)
                values = pltpu.roll(values, shift, 2)
                chosen = wanted & (group == side) & (parity == i) & (tile >= 0)
                total = jnp.where(chosen[None], values, total)
    for k in range(levels):
        arriving_ref[8 * k : 8 * k + 8] = total[k]
    returned = split_dot(arriving_ref[...], place_ref[...])
    depth = four_times(lc_ref[...])
    for k in range(levels):
        result = base_ref[k][:, :cells] + jnp.where(
            k < depth, returned[8 * k : 8 * k + 8, :cells], 0.0
        )
        for n in range(4):
            out_ref[k, n] = result[2 * n : 2 * n + 2]


def shards_fast(
    cotangent,
    courant_x,
    courant_y,
    diffusivity,
    vert_diff,
    level_count,
    edge_tile,
    edge_code,
    corner_tile,
    corner_code,
):
    levels, tracers, tiles_here, cells = cotangent.shape
    count = lax.axis_size("tile")
    vmem = pl.BlockSpec(memory_space=pltpu.VMEM)
    smem = pl.BlockSpec(memory_space=pltpu.SMEM)
    hbm = pl.BlockSpec(memory_space=pltpu.HBM)
    base, strips = pl.pallas_call(
        solve_kernel,
        name="solve",
        out_shape=(
            jax.ShapeDtypeStruct((levels, 8, PADDED), jnp.float32),
            jax.ShapeDtypeStruct((levels, 8, 128), jnp.float32),
        ),
        in_specs=[hbm] * 8,
        out_specs=(vmem, vmem),
        scratch_shapes=[
            pltpu.VMEM((levels, 8, cells), jnp.float32),
            pltpu.VMEM((levels, 8, cells), jnp.float32),
            pltpu.VMEM((8 * levels, PADDED + 128), jnp.float32),
            pltpu.SMEM(edge_code.shape, jnp.int32),
            pltpu.VMEM(cotangent.shape, jnp.float32),
            pltpu.VMEM(courant_x.shape, jnp.float32),
            pltpu.VMEM(courant_y.shape, jnp.float32),
            pltpu.VMEM(diffusivity.shape, jnp.float32),
            pltpu.VMEM(vert_diff.shape, jnp.float32),
            pltpu.VMEM(level_count.shape, jnp.int32),
            pltpu.VMEM((PADDED + 128, 256), jnp.bfloat16),
            pltpu.SemaphoreType.DMA((8,)),
        ],
        compiler_params=pltpu.CompilerParams(vmem_limit_bytes=62 << 20),
    )(edge_code, cotangent, courant_x, courant_y, diffusivity, vert_diff, level_count, strip_selector())
    near = pl.pallas_call(
        functools.partial(send_kernel, count),
        name="send",
        out_shape=jax.ShapeDtypeStruct((2 * PLANE + 1, 2, levels, 8, 128), jnp.float32),
        in_specs=[hbm],
        out_specs=hbm,
        scratch_shapes=[
            pltpu.SemaphoreType.DMA,
            pltpu.SemaphoreType.DMA((4 * PLANE + 1,)),
            pltpu.SemaphoreType.DMA((2 * PLANE + 1, 2)),
        ],
        compiler_params=pltpu.CompilerParams(collective_id=0, has_side_effects=True),
    )(strips)
    return pl.pallas_call(
        functools.partial(place_kernel, count),
        name="place",
        out_shape=jax.ShapeDtypeStruct(cotangent.shape, jnp.float32),
        in_specs=[smem] * 4 + [vmem] * 4,
        out_specs=vmem,
        scratch_shapes=[pltpu.VMEM((8 * levels, 128), jnp.float32)],
        compiler_params=pltpu.CompilerParams(vmem_limit_bytes=40 << 20),
    )(edge_tile, edge_code, corner_tile, corner_code, near, base, level_count, strip_placer())


def solution(mesh):
    placed = (
        P("lev", None, "tile", None),
        P("lev", "tile", None),
        P("lev", "tile", None),
        P("tile", None),
        P("lev", "tile", None),
        P("tile", None),
        P("tile", None),
        P("tile", None),
        P("tile", None),
        P("tile", None),
    )
    fast = mesh.shape["lev"] == 1 and mesh.shape["tile"] % 8 == 0 and mesh.shape["tile"] > 2 * BAND
    return jax.shard_map(
        shards_fast if fast else shards, mesh=mesh, in_specs=placed, out_specs=P("lev", None, "tile", None), check_vma=False
    )
```

```python
import functools

import jax
import jax.numpy as jnp
import numpy as np
from jax import lax
from jax.experimental import pallas as pl
from jax.experimental.pallas import tpu as pltpu
from jax.sharding import PartitionSpec as P

EDGE = 30
BAND = 8


stencil_offsets = [(0, -1), (0, 1), (-1, 0), (1, 0), (-1, -1), (-1, 1), (1, -1), (1, 1)]


def from_behind(value, axis, steps):
    count = lax.axis_size(axis)
    initial, last = (max(0, -steps), min(count, count - steps))
    return lax.ppermute(value, axis, [(source, source + steps) for source in range(initial, last)])


def shifted_2(value, axis, by):
    devices = lax.axis_size(axis)
    return lax.ppermute(value, axis, [(i, (i + by) % devices) for i in range(devices)])


def stencil_weights(diffuse, flow_x, flow_y):
    return [
        diffuse + 0.5 * flow_x,
        diffuse - 0.5 * flow_x,
        diffuse + 0.5 * flow_y,
        diffuse - 0.5 * flow_y,
        0.25 * diffuse,
        0.25 * diffuse,
        0.25 * diffuse,
        0.25 * diffuse,
    ]


def eliminate(right_side, coupling_up, coupling_down, initial):

    def advance(state, inputs):
        factor, partial_value = state
        source, upper_term, lower_term = inputs
        divisor = 1.0 + upper_term + lower_term + upper_term * factor
        factor_new = -lower_term / divisor
        partial_new = (source + upper_term * partial_value) / divisor
        return ((factor_new, partial_new), (factor_new, partial_new))

    final_state, outputs = lax.scan(advance, initial, (right_side, coupling_up, coupling_down))
    return outputs


def substitute(factors, partials, below_field):

    def backward(state, inputs):
        factor, partial_value = inputs
        column_value = partial_value - factor * state
        return (column_value, column_value)

    final_state, fields = lax.scan(backward, below_field, (factors, partials), reverse=True)
    return fields


def cycle_tables():
    padded_edge = EDGE + 2
    cycle_spots = []
    cell_spots = []
    for border in range(4):
        for position in range(EDGE):
            if border == 0:
                cycle_spots.append(position + 1)
                cell_spots.append(position)
            elif border == 1:
                cycle_spots.append((padded_edge - 1) * padded_edge + position + 1)
                cell_spots.append((EDGE - 1) * EDGE + position)
            elif border == 2:
                cycle_spots.append((position + 1) * padded_edge)
                cell_spots.append(position * EDGE)
            else:
                cycle_spots.append((position + 1) * padded_edge + padded_edge - 1)
                cell_spots.append(position * EDGE + EDGE - 1)
    cycle_spots += [
        0,
        padded_edge - 1,
        (padded_edge - 1) * padded_edge,
        padded_edge * padded_edge - 1,
    ]
    cell_spots += [0, EDGE - 1, (EDGE - 1) * EDGE, EDGE * EDGE - 1]
    placing = np.zeros((len(cycle_spots), EDGE * EDGE), np.float32)
    placing[np.arange(len(cycle_spots)), np.array(cell_spots)] = 1.0
    return (np.array(cycle_spots, np.int32), placing)


def embed(field):
    leading = field.shape[:-1]
    square = field.reshape(leading + (EDGE, EDGE))
    padded = jnp.pad(square, [(0, 0)] * len(leading) + [(1, 1), (1, 1)])
    return padded.reshape(leading + ((EDGE + 2) * (EDGE + 2),))


def shards(
    cotangent,
    courant_x,
    courant_y,
    diffusivity,
    vert_diff,
    level_count,
    edge_tile,
    edge_code,
    corner_tile,
    corner_code,
):
    levels_here = cotangent.shape[0]
    tracers = cotangent.shape[1]
    tiles_here = cotangent.shape[2]
    cells = cotangent.shape[3]
    padded_edge = EDGE + 2
    cycle_size = 4 * EDGE + 4
    lev_count = lax.axis_size("lev")
    depth_index = (
        lax.axis_index("lev") * levels_here
        + jnp.arange(levels_here, dtype=jnp.int32)[:, None, None]
    )
    wet_mask = (depth_index < level_count[None]).astype(jnp.float32)
    coupling = jnp.where(depth_index == 0, jnp.float32(0.0), vert_diff * wet_mask)
    deeper = from_behind(coupling[0], "lev", -1)
    coupling_down = jnp.concatenate([coupling[1:], deeper[None]], axis=0)[:, None]
    coupling_up = coupling[:, None]
    initial = (
        jnp.zeros((1, tiles_here, cells), jnp.float32),
        jnp.zeros((tracers, tiles_here, cells), jnp.float32),
    )
    for sweep_index in range(lev_count - 1):
        factors, partials = eliminate(cotangent, coupling_up, coupling_down, initial)
        initial = from_behind((factors[-1], partials[-1]), "lev", 1)
    factors, partials = eliminate(cotangent, coupling_up, coupling_down, initial)
    below_field = jnp.zeros((tracers, tiles_here, cells), jnp.float32)
    for sweep_index in range(lev_count - 1):
        fields = substitute(factors, partials, below_field)
        below_field = from_behind(fields[0], "lev", -1)
    solved = substitute(factors, partials, below_field)
    weighted = solved * wet_mask[:, None]
    weighted_ext = embed(weighted)
    diffuse_ext = embed(diffusivity)[None, None]
    flow_x_ext = embed(courant_x)[:, None]
    flow_y_ext = embed(courant_y)[:, None]
    weights = stencil_weights(diffuse_ext, flow_x_ext, flow_y_ext)
    leading = weighted_ext.shape[:-1]
    spread = jnp.zeros_like(weighted_ext)
    for (shift_row, shift_col), weight in zip(stencil_offsets, weights):
        contribution = weight * weighted_ext
        offset = shift_row * padded_edge + shift_col
        if offset > 0:
            shifted = jnp.concatenate(
                [jnp.zeros(leading + (offset,), jnp.float32), contribution[..., :-offset]], axis=-1
            )
        else:
            shifted = jnp.concatenate(
                [contribution[..., -offset:], jnp.zeros(leading + (-offset,), jnp.float32)], axis=-1
            )
        spread = spread + shifted
    cycle_spots, placing = cycle_tables()
    outgoing = jnp.take(spread, jnp.asarray(cycle_spots), axis=3)
    interior = spread.reshape(leading + (padded_edge, padded_edge))[..., 1:-1, 1:-1].reshape(
        solved.shape
    )
    partners = jnp.concatenate([edge_tile, corner_tile], axis=1)

    def collect(gathered_sum, portion, first_tile):
        tile_span = portion.shape[2]
        onehot = (
            partners[:, :, None]
            == first_tile + jnp.arange(tile_span, dtype=jnp.int32)[None, None, :]
        ).astype(jnp.float32)
        return gathered_sum + jnp.einsum(
            "tkw,dnwr->dntkr", onehot, portion, precision=lax.Precision.HIGHEST
        )

    tile_count = lax.axis_size("tile")
    own_index = lax.axis_index("tile")
    reach = (2 * BAND + tiles_here - 1) // tiles_here
    fetched = collect(
        jnp.zeros((levels_here, tracers, tiles_here, 8, cycle_size), jnp.float32),
        outgoing,
        own_index * tiles_here,
    )
    for distance in range(-reach, reach + 1):
        if distance != 0:
            portion = shifted_2(outgoing, "tile", distance)
            source = (own_index - distance) % tile_count
            fetched = collect(fetched, portion, source * tiles_here)
    side_values = fetched[:, :, :, :4, : 4 * EDGE].reshape(
        levels_here, tracers, tiles_here, 4, 4, EDGE
    )
    side_choice = (
        (edge_code % 4)[:, :, None] == jnp.arange(4, dtype=jnp.int32)[None, None, :]
    ).astype(jnp.float32)
    strips = jnp.sum(side_values * side_choice[None, None, :, :, :, None], axis=4)
    strips = jnp.where((edge_code >= 4)[None, None, :, :, None], strips[..., ::-1], strips)
    corner_values = fetched[:, :, :, 4:, 4 * EDGE :]
    corner_choice = (
        corner_code[:, :, None] == jnp.arange(4, dtype=jnp.int32)[None, None, :]
    ).astype(jnp.float32)
    corner_picked = jnp.sum(corner_values * corner_choice[None, None], axis=4)
    arriving = jnp.concatenate(
        [strips.reshape(levels_here, tracers, tiles_here, 4 * EDGE), corner_picked], axis=3
    )
    returned = jnp.einsum(
        "dntr,rc->dntc", arriving, jnp.asarray(placing), precision=lax.Precision.HIGHEST
    )
    diffuse_here = diffusivity[None, None]
    return wet_mask[:, None] * ((1.0 - 5.0 * diffuse_here) * weighted + interior + returned)


PADDED = 1024
SIDE_LANES = 32
PLANE = 4
CHUNKS = 4
MESH = pl.DeviceIdType.MESH


def strip_selector():
    chosen = np.zeros((PADDED + 128, 256), np.float32)
    for j in range(EDGE):
        for side, lane in enumerate([PADDED - EDGE + j, EDGE * EDGE + j, EDGE * j, EDGE * j + EDGE - 1]):
            chosen[lane, SIDE_LANES * side + j] = 1.0
            chosen[lane, 128 + SIDE_LANES * side + EDGE - 1 - j] = 1.0
    for corner, cell in enumerate([0, EDGE - 1, (EDGE - 1) * EDGE, EDGE * EDGE - 1]):
        chosen[PADDED + cell % 128, SIDE_LANES * corner + EDGE] = 1.0
    return jnp.asarray(chosen, jnp.bfloat16)


def strip_placer():
    placing = np.zeros((128, PADDED), np.float32)
    for j in range(EDGE):
        for side, cell in enumerate([j, (EDGE - 1) * EDGE + j, EDGE * j, EDGE * j + EDGE - 1]):
            placing[SIDE_LANES * side + j, cell] = 1.0
    for corner, cell in enumerate([0, EDGE - 1, (EDGE - 1) * EDGE, EDGE * EDGE - 1]):
        placing[SIDE_LANES * corner + EDGE, cell] = 1.0
    return jnp.asarray(placing, jnp.bfloat16)


def split_dot(left, right):
    high = left.astype(jnp.bfloat16)
    low = (left - high.astype(jnp.float32)).astype(jnp.bfloat16)
    return jnp.dot(high, right, preferred_element_type=jnp.float32) + jnp.dot(
        low, right, preferred_element_type=jnp.float32
    )


def four_times(pair):
    return jnp.concatenate([pair, pair, pair, pair], axis=0)


def widen(rows):
    return jnp.concatenate(
        [rows, jnp.zeros((rows.shape[0], PADDED - rows.shape[1]), rows.dtype)], axis=1
    )


def solve_kernel(
    code_hbm, cot_hbm, cx_hbm, cy_hbm, dif_hbm, vd_hbm, lc_hbm, sel_hbm,
    base_hbm, strips_ref, base_ref, factor_ref, partial_ref, edge_ref,
    code_ref, cot_ref, cx_ref, cy_ref, dif_ref, vd_ref, lc_ref, sel_ref, sems,
):
    levels = cot_ref.shape[0]
    cells = cot_ref.shape[3]
    pairs = [
        (lc_hbm, lc_ref),
        (vd_hbm, vd_ref),
        (dif_hbm, dif_ref),
        (cx_hbm, cx_ref),
        (cy_hbm, cy_ref),
        (code_hbm, code_ref),
        (sel_hbm, sel_ref),
    ]
    copies = [
        pltpu.make_async_copy(source, target, sems.at[i])
        for i, (source, target) in enumerate(pairs)
    ]
    chunk = levels // CHUNKS
    arrivals = [
        pltpu.make_async_copy(
            cot_hbm.at[c * chunk : (c + 1) * chunk],
            cot_ref.at[c * chunk : (c + 1) * chunk],
            sems.at[len(pairs) + c],
        )
        for c in range(CHUNKS)
    ]
    leaving = [
        pltpu.make_async_copy(
            base_ref.at[c * chunk : (c + 1) * chunk],
            base_hbm.at[c * chunk : (c + 1) * chunk],
            sems.at[len(pairs) + CHUNKS + c],
        )
        for c in range(CHUNKS)
    ]
    for copy in copies[:2] + arrivals + copies[2:]:
        copy.start()
    for copy in copies[:2]:
        copy.wait()
    depth = four_times(lc_ref[...])

    def coupling(k):
        if k == 0 or k == levels:
            return jnp.zeros((8, cells), jnp.float32)
        return jnp.where(k < depth, four_times(vd_ref[k]), 0.0)

    factor = jnp.zeros((8, cells), jnp.float32)
    partial_value = jnp.zeros((8, cells), jnp.float32)
    upper = coupling(0)
    for k in range(levels):
        if k % chunk == 0:
            arrivals[k // chunk].wait()
        lower = coupling(k + 1)
        source = jnp.concatenate([cot_ref[k, n] for n in range(4)], axis=0)
        inverse = 1.0 / ((1.0 + upper + lower) + upper * factor)
        factor = -lower * inverse
        partial_value = (source + upper * partial_value) * inverse
        factor_ref[k] = factor
        partial_ref[k] = partial_value
        upper = lower

    lane = lax.broadcasted_iota(jnp.int32, (8, PADDED), 1)
    row_lane = jnp.where(lane >= PADDED - EDGE, lane - (PADDED - EDGE), lane)
    column = lax.rem(row_lane, EDGE)
    first = column == 0
    last = column == EDGE - 1
    inside = lane < cells
    short = lax.broadcasted_iota(jnp.int32, (8, 128), 1)
    corner_0 = (short == 0) | (short == EDGE - 1)
    corner_6 = short == ((EDGE - 1) * EDGE) % 128
    corner_7 = short == (EDGE * EDGE - 1) % 128
    for copy in copies[2:5]:
        copy.wait()
    diffuse = widen(four_times(dif_ref[...]))
    quarter = 0.25 * diffuse
    centre = 1.0 - 5.0 * diffuse
    wide_depth = widen(depth)
    solved = jnp.zeros((8, cells), jnp.float32)
    for k in reversed(range(levels)):
        solved = partial_ref[k] - factor_ref[k] * solved
        u = widen(jnp.where(k < depth, solved, 0.0))
        half_x = 0.5 * widen(four_times(cx_ref[k]))
        half_y = 0.5 * widen(four_times(cy_ref[k]))
        diagonal = quarter * u
        both = pltpu.roll(diagonal, EDGE, 1) + pltpu.roll(diagonal, PADDED - EDGE, 1)
        west = both + (diffuse + half_x) * u
        east = both + (diffuse - half_x) * u
        spread = pltpu.roll((diffuse + half_y) * u, PADDED - EDGE, 1)
        spread = spread + pltpu.roll((diffuse - half_y) * u, EDGE, 1)
        spread = spread + pltpu.roll(jnp.where(first, 0.0, west), PADDED - 1, 1)
        spread = spread + pltpu.roll(jnp.where(last, 0.0, east), 1, 1)
        base_ref[k] = jnp.where(k < wide_depth, centre * u + spread, 0.0)
        edge_ref[8 * k : 8 * k + 8, :PADDED] = jnp.where(
            inside, jnp.where(first, west, east), spread
        )
        edge_ref[8 * k : 8 * k + 8, PADDED:] = (
            jnp.where(corner_0, diagonal[:, 0:128], 0.0)
            + jnp.where(corner_6, diagonal[:, 768:896], 0.0)
            + jnp.where(corner_7, diagonal[:, 896:1024], 0.0)
        )
        if k % chunk == 0:
            leaving[k // chunk].start()
    for copy in copies[5:]:
        copy.wait()
    both_ways = split_dot(edge_ref[...], sel_ref[...])
    parity = lax.rem(lax.broadcasted_iota(jnp.int32, (8, 128), 0), 2)
    code = jnp.zeros((8, 128), jnp.int32)
    for i in range(2):
        for side in range(4):
            code = jnp.where((parity == i) & (short // SIDE_LANES == side), code_ref[i, side], code)
    flipped = (code >= 4) & (lax.rem(short, SIDE_LANES) < EDGE)
    for k in range(levels):
        rows = both_ways[8 * k : 8 * k + 8]
        strips_ref[k] = jnp.where(flipped, rows[:, 128:], rows[:, :128])
    for copy in leaving:
        copy.wait()


def send_kernel(count, strips_ref, near_ref, own_sem, send_sem, recv_sem):
    chips = count // 2
    me = lax.axis_index("tile")
    chip = me // 2
    core = lax.rem(me, 2)
    place = lax.rem(chip, PLANE)

    def at(steps):
        return 2 * lax.rem(chip + steps + chips, chips) + core

    partner = me + 1 - 2 * core
    wraps = [(place + j) // PLANE for j in range(PLANE)]
    beside = [at(j - PLANE * wraps[j]) for j in range(PLANE)]
    above, below = at(PLANE), at(-PLANE)
    barrier = pltpu.get_barrier_semaphore()
    peers = [partner, above, below] + beside[1:]
    for peer in peers:
        pl.semaphore_signal(barrier, inc=1, device_id={"tile": peer}, device_id_type=MESH)
    own = pltpu.make_async_copy(strips_ref, near_ref.at[PLANE, core], own_sem)
    own.start()
    pl.semaphore_wait(barrier, len(peers))
    copies = []

    def send(source, spot, to):
        copy = pltpu.make_async_remote_copy(
            src_ref=source,
            dst_ref=near_ref.at[spot, core],
            send_sem=send_sem.at[len(copies)],
            recv_sem=recv_sem.at[spot, core],
            device_id={"tile": to},
            device_id_type=MESH,
        )
        copy.start()
        copies.append(copy)

    def arrived(spot, side):
        pltpu.make_async_remote_copy(
            src_ref=strips_ref,
            dst_ref=near_ref.at[spot, side],
            send_sem=own_sem,
            recv_sem=recv_sem.at[spot, side],
            device_id={"tile": partner},
            device_id_type=MESH,
        ).wait_recv()

    def share(spot):
        send(near_ref.at[spot, core], spot, partner)

    send(strips_ref, 0, above)
    send(strips_ref, 2 * PLANE, below)
    for j in range(1, PLANE):
        send(strips_ref, PLANE - j + PLANE * wraps[j], beside[j])
    send(strips_ref, PLANE, partner)
    arrived(0, core)
    arrived(2 * PLANE, core)
    for j in range(1, PLANE):
        source = near_ref.at[2 * PLANE - 2 * PLANE * wraps[j], core]
        send(source, 2 * PLANE - PLANE * wraps[j] - j, beside[j])
    share(0)
    share(2 * PLANE)
    for j in range(1, PLANE):
        spot = PLANE + j - PLANE * wraps[j]
        arrived(spot, core)
        share(spot)
    for j in range(1, PLANE):
        spot = j + PLANE * wraps[j]
        arrived(spot, core)
        share(spot)
    for spot in range(2 * PLANE + 1):
        arrived(spot, 1 - core)
    own.wait()
    for copy in copies:
        copy.wait_send()


def place_kernel(
    count, et_hbm, ec_hbm, ct_hbm, cc_hbm, near_hbm, base_hbm, lc_hbm, place_hbm,
    out_hbm, et_ref, ec_ref, ct_ref, cc_ref, base_ref, lc_ref, place_ref, block_ref,
    arriving_ref, out_ref, sems, block_sems, out_sems,
):
    levels = base_ref.shape[0]
    cells = out_ref.shape[3]
    me = lax.axis_index("tile")
    pairs = [
        (et_hbm, et_ref),
        (ec_hbm, ec_ref),
        (ct_hbm, ct_ref),
        (cc_hbm, cc_ref),
        (place_hbm, place_ref),
        (lc_hbm, lc_ref),
        (base_hbm, base_ref),
    ]
    copies = [
        pltpu.make_async_copy(source, target, sems.at[i])
        for i, (source, target) in enumerate(pairs)
    ]
    for copy in copies[:4]:
        copy.start()
    lane = lax.broadcasted_iota(jnp.int32, (8, 128), 1)
    parity = lax.rem(lax.broadcasted_iota(jnp.int32, (8, 128), 0), 2)
    group = lane // SIDE_LANES
    spot = lax.rem(lane, SIDE_LANES)
    for copy in copies[:4]:
        copy.wait()
    units = [
        (i, side, tiles_ref, codes_ref, wanted)
        for tiles_ref, codes_ref, wanted in (
            (et_ref, ec_ref, spot < EDGE),
            (ct_ref, cc_ref, spot == EDGE),
        )
        for i in range(2)
        for side in range(4)
    ]
    blocks = []
    for index, (i, side, tiles_ref, codes_ref, wanted) in enumerate(units):
        tile = tiles_ref[i, side]
        there = jnp.maximum(tile, 0)
        slot = lax.rem(there // 4 - me // 2 + PLANE + count // 2, count // 2)
        slot = jnp.where(tile < 0, PLANE, slot)
        block = pltpu.make_async_copy(
            near_hbm.at[slot, lax.rem(there // 2, 2)], block_ref.at[index], block_sems.at[index]
        )
        block.start()
        blocks.append(block)
    for copy in copies[4:]:
        copy.start()
    total = jnp.zeros((levels, 8, 128), jnp.float32)
    for index, (i, side, tiles_ref, codes_ref, wanted) in enumerate(units):
        tile = tiles_ref[i, side]
        there = jnp.maximum(tile, 0)
        blocks[index].wait()
        values = block_ref[index]
        values = jnp.where(
            lax.rem(there, 2) == i, values, pltpu.roll(values, 1 if i == 1 else 7, 1)
        )
        shift = lax.rem(SIDE_LANES * (side - lax.rem(codes_ref[i, side], 4)) + 128, 128)
        values = pltpu.roll(values, shift, 2)
        chosen = wanted & (group == side) & (parity == i) & (tile >= 0)
        total = jnp.where(chosen[None], values, total)
    for k in range(levels):
        arriving_ref[8 * k : 8 * k + 8] = total[k]
    for copy in copies[4:]:
        copy.wait()
    depth = four_times(lc_ref[...])
    chunk = levels // CHUNKS
    leaving = []
    for c in range(CHUNKS):
        here = slice(c * chunk, (c + 1) * chunk)
        returned = split_dot(arriving_ref[8 * c * chunk : 8 * (c + 1) * chunk], place_ref[...])
        for k in range(c * chunk, (c + 1) * chunk):
            row = 8 * (k - c * chunk)
            result = base_ref[k][:, :cells] + jnp.where(
                k < depth, returned[row : row + 8, :cells], 0.0
            )
            for n in range(4):
                out_ref[k, n] = result[2 * n : 2 * n + 2]
        copy = pltpu.make_async_copy(out_ref.at[here], out_hbm.at[here], out_sems.at[c])
        copy.start()
        leaving.append(copy)
    for copy in leaving:
        copy.wait()


def shards_fast(
    cotangent,
    courant_x,
    courant_y,
    diffusivity,
    vert_diff,
    level_count,
    edge_tile,
    edge_code,
    corner_tile,
    corner_code,
):
    levels, tracers, tiles_here, cells = cotangent.shape
    count = lax.axis_size("tile")
    vmem = pl.BlockSpec(memory_space=pltpu.VMEM)
    hbm = pl.BlockSpec(memory_space=pltpu.HBM)
    base, strips = pl.pallas_call(
        solve_kernel,
        name="solve",
        out_shape=(
            jax.ShapeDtypeStruct((levels, 8, PADDED), jnp.float32),
            jax.ShapeDtypeStruct((levels, 8, 128), jnp.float32),
        ),
        in_specs=[hbm] * 8,
        out_specs=(hbm, vmem),
        scratch_shapes=[
            pltpu.VMEM((levels, 8, PADDED), jnp.float32),
            pltpu.VMEM((levels, 8, cells), jnp.float32),
            pltpu.VMEM((levels, 8, cells), jnp.float32),
            pltpu.VMEM((8 * levels, PADDED + 128), jnp.float32),
            pltpu.SMEM(edge_code.shape, jnp.int32),
            pltpu.VMEM(cotangent.shape, jnp.float32),
            pltpu.VMEM(courant_x.shape, jnp.float32),
            pltpu.VMEM(courant_y.shape, jnp.float32),
            pltpu.VMEM(diffusivity.shape, jnp.float32),
            pltpu.VMEM(vert_diff.shape, jnp.float32),
            pltpu.VMEM(level_count.shape, jnp.int32),
            pltpu.VMEM((PADDED + 128, 256), jnp.bfloat16),
            pltpu.SemaphoreType.DMA((7 + 2 * CHUNKS,)),
        ],
        compiler_params=pltpu.CompilerParams(vmem_limit_bytes=62 << 20),
    )(edge_code, cotangent, courant_x, courant_y, diffusivity, vert_diff, level_count, strip_selector())
    near = pl.pallas_call(
        functools.partial(send_kernel, count),
        name="send",
        out_shape=jax.ShapeDtypeStruct((2 * PLANE + 1, 2, levels, 8, 128), jnp.float32),
        in_specs=[hbm],
        out_specs=hbm,
        scratch_shapes=[
            pltpu.SemaphoreType.DMA,
            pltpu.SemaphoreType.DMA((4 * PLANE + 1,)),
            pltpu.SemaphoreType.DMA((2 * PLANE + 1, 2)),
        ],
        compiler_params=pltpu.CompilerParams(collective_id=0, has_side_effects=True),
    )(strips)
    return pl.pallas_call(
        functools.partial(place_kernel, count),
        name="place",
        out_shape=jax.ShapeDtypeStruct(cotangent.shape, jnp.float32),
        in_specs=[hbm] * 8,
        out_specs=hbm,
        scratch_shapes=[pltpu.SMEM(edge_tile.shape, jnp.int32)] * 4
        + [
            pltpu.VMEM((levels, 8, PADDED), jnp.float32),
            pltpu.VMEM(level_count.shape, jnp.int32),
            pltpu.VMEM((128, PADDED), jnp.bfloat16),
            pltpu.VMEM((16, levels, 8, 128), jnp.float32),
            pltpu.VMEM((8 * levels, 128), jnp.float32),
            pltpu.VMEM(cotangent.shape, jnp.float32),
            pltpu.SemaphoreType.DMA((7,)),
            pltpu.SemaphoreType.DMA((16,)),
            pltpu.SemaphoreType.DMA((CHUNKS,)),
        ],
        compiler_params=pltpu.CompilerParams(vmem_limit_bytes=62 << 20),
    )(edge_tile, edge_code, corner_tile, corner_code, near, base, level_count, strip_placer())


def solution(mesh):
    placed = (
        P("lev", None, "tile", None),
        P("lev", "tile", None),
        P("lev", "tile", None),
        P("tile", None),
        P("lev", "tile", None),
        P("tile", None),
        P("tile", None),
        P("tile", None),
        P("tile", None),
        P("tile", None),
    )
    fast = mesh.shape["lev"] == 1 and mesh.shape["tile"] % 8 == 0 and mesh.shape["tile"] > 2 * BAND
    return jax.shard_map(
        shards_fast if fast else shards, mesh=mesh, in_specs=placed, out_specs=P("lev", None, "tile", None), check_vma=False
    )
```

```python
import functools

import jax
import jax.numpy as jnp
import numpy as np
from jax import lax
from jax.experimental import pallas as pl
from jax.experimental.pallas import tpu as pltpu
from jax.sharding import PartitionSpec as P

EDGE = 30
BAND = 8


stencil_offsets = [(0, -1), (0, 1), (-1, 0), (1, 0), (-1, -1), (-1, 1), (1, -1), (1, 1)]


def from_behind(value, axis, steps):
    count = lax.axis_size(axis)
    initial, last = (max(0, -steps), min(count, count - steps))
    return lax.ppermute(value, axis, [(source, source + steps) for source in range(initial, last)])


def shifted_2(value, axis, by):
    devices = lax.axis_size(axis)
    return lax.ppermute(value, axis, [(i, (i + by) % devices) for i in range(devices)])


def stencil_weights(diffuse, flow_x, flow_y):
    return [
        diffuse + 0.5 * flow_x,
        diffuse - 0.5 * flow_x,
        diffuse + 0.5 * flow_y,
        diffuse - 0.5 * flow_y,
        0.25 * diffuse,
        0.25 * diffuse,
        0.25 * diffuse,
        0.25 * diffuse,
    ]


def eliminate(right_side, coupling_up, coupling_down, initial):

    def advance(state, inputs):
        factor, partial_value = state
        source, upper_term, lower_term = inputs
        divisor = 1.0 + upper_term + lower_term + upper_term * factor
        factor_new = -lower_term / divisor
        partial_new = (source + upper_term * partial_value) / divisor
        return ((factor_new, partial_new), (factor_new, partial_new))

    final_state, outputs = lax.scan(advance, initial, (right_side, coupling_up, coupling_down))
    return outputs


def substitute(factors, partials, below_field):

    def backward(state, inputs):
        factor, partial_value = inputs
        column_value = partial_value - factor * state
        return (column_value, column_value)

    final_state, fields = lax.scan(backward, below_field, (factors, partials), reverse=True)
    return fields


def cycle_tables():
    padded_edge = EDGE + 2
    cycle_spots = []
    cell_spots = []
    for border in range(4):
        for position in range(EDGE):
            if border == 0:
                cycle_spots.append(position + 1)
                cell_spots.append(position)
            elif border == 1:
                cycle_spots.append((padded_edge - 1) * padded_edge + position + 1)
                cell_spots.append((EDGE - 1) * EDGE + position)
            elif border == 2:
                cycle_spots.append((position + 1) * padded_edge)
                cell_spots.append(position * EDGE)
            else:
                cycle_spots.append((position + 1) * padded_edge + padded_edge - 1)
                cell_spots.append(position * EDGE + EDGE - 1)
    cycle_spots += [
        0,
        padded_edge - 1,
        (padded_edge - 1) * padded_edge,
        padded_edge * padded_edge - 1,
    ]
    cell_spots += [0, EDGE - 1, (EDGE - 1) * EDGE, EDGE * EDGE - 1]
    placing = np.zeros((len(cycle_spots), EDGE * EDGE), np.float32)
    placing[np.arange(len(cycle_spots)), np.array(cell_spots)] = 1.0
    return (np.array(cycle_spots, np.int32), placing)


def embed(field):
    leading = field.shape[:-1]
    square = field.reshape(leading + (EDGE, EDGE))
    padded = jnp.pad(square, [(0, 0)] * len(leading) + [(1, 1), (1, 1)])
    return padded.reshape(leading + ((EDGE + 2) * (EDGE + 2),))


def shards(
    cotangent,
    courant_x,
    courant_y,
    diffusivity,
    vert_diff,
    level_count,
    edge_tile,
    edge_code,
    corner_tile,
    corner_code,
):
    levels_here = cotangent.shape[0]
    tracers = cotangent.shape[1]
    tiles_here = cotangent.shape[2]
    cells = cotangent.shape[3]
    padded_edge = EDGE + 2
    cycle_size = 4 * EDGE + 4
    lev_count = lax.axis_size("lev")
    depth_index = (
        lax.axis_index("lev") * levels_here
        + jnp.arange(levels_here, dtype=jnp.int32)[:, None, None]
    )
    wet_mask = (depth_index < level_count[None]).astype(jnp.float32)
    coupling = jnp.where(depth_index == 0, jnp.float32(0.0), vert_diff * wet_mask)
    deeper = from_behind(coupling[0], "lev", -1)
    coupling_down = jnp.concatenate([coupling[1:], deeper[None]], axis=0)[:, None]
    coupling_up = coupling[:, None]
    initial = (
        jnp.zeros((1, tiles_here, cells), jnp.float32),
        jnp.zeros((tracers, tiles_here, cells), jnp.float32),
    )
    for sweep_index in range(lev_count - 1):
        factors, partials = eliminate(cotangent, coupling_up, coupling_down, initial)
        initial = from_behind((factors[-1], partials[-1]), "lev", 1)
    factors, partials = eliminate(cotangent, coupling_up, coupling_down, initial)
    below_field = jnp.zeros((tracers, tiles_here, cells), jnp.float32)
    for sweep_index in range(lev_count - 1):
        fields = substitute(factors, partials, below_field)
        below_field = from_behind(fields[0], "lev", -1)
    solved = substitute(factors, partials, below_field)
    weighted = solved * wet_mask[:, None]
    weighted_ext = embed(weighted)
    diffuse_ext = embed(diffusivity)[None, None]
    flow_x_ext = embed(courant_x)[:, None]
    flow_y_ext = embed(courant_y)[:, None]
    weights = stencil_weights(diffuse_ext, flow_x_ext, flow_y_ext)
    leading = weighted_ext.shape[:-1]
    spread = jnp.zeros_like(weighted_ext)
    for (shift_row, shift_col), weight in zip(stencil_offsets, weights):
        contribution = weight * weighted_ext
        offset = shift_row * padded_edge + shift_col
        if offset > 0:
            shifted = jnp.concatenate(
                [jnp.zeros(leading + (offset,), jnp.float32), contribution[..., :-offset]], axis=-1
            )
        else:
            shifted = jnp.concatenate(
                [contribution[..., -offset:], jnp.zeros(leading + (-offset,), jnp.float32)], axis=-1
            )
        spread = spread + shifted
    cycle_spots, placing = cycle_tables()
    outgoing = jnp.take(spread, jnp.asarray(cycle_spots), axis=3)
    interior = spread.reshape(leading + (padded_edge, padded_edge))[..., 1:-1, 1:-1].reshape(
        solved.shape
    )
    partners = jnp.concatenate([edge_tile, corner_tile], axis=1)

    def collect(gathered_sum, portion, first_tile):
        tile_span = portion.shape[2]
        onehot = (
            partners[:, :, None]
            == first_tile + jnp.arange(tile_span, dtype=jnp.int32)[None, None, :]
        ).astype(jnp.float32)
        return gathered_sum + jnp.einsum(
            "tkw,dnwr->dntkr", onehot, portion, precision=lax.Precision.HIGHEST
        )

    tile_count = lax.axis_size("tile")
    own_index = lax.axis_index("tile")
    reach = (2 * BAND + tiles_here - 1) // tiles_here
    fetched = collect(
        jnp.zeros((levels_here, tracers, tiles_here, 8, cycle_size), jnp.float32),
        outgoing,
        own_index * tiles_here,
    )
    for distance in range(-reach, reach + 1):
        if distance != 0:
            portion = shifted_2(outgoing, "tile", distance)
            source = (own_index - distance) % tile_count
            fetched = collect(fetched, portion, source * tiles_here)
    side_values = fetched[:, :, :, :4, : 4 * EDGE].reshape(
        levels_here, tracers, tiles_here, 4, 4, EDGE
    )
    side_choice = (
        (edge_code % 4)[:, :, None] == jnp.arange(4, dtype=jnp.int32)[None, None, :]
    ).astype(jnp.float32)
    strips = jnp.sum(side_values * side_choice[None, None, :, :, :, None], axis=4)
    strips = jnp.where((edge_code >= 4)[None, None, :, :, None], strips[..., ::-1], strips)
    corner_values = fetched[:, :, :, 4:, 4 * EDGE :]
    corner_choice = (
        corner_code[:, :, None] == jnp.arange(4, dtype=jnp.int32)[None, None, :]
    ).astype(jnp.float32)
    corner_picked = jnp.sum(corner_values * corner_choice[None, None], axis=4)
    arriving = jnp.concatenate(
        [strips.reshape(levels_here, tracers, tiles_here, 4 * EDGE), corner_picked], axis=3
    )
    returned = jnp.einsum(
        "dntr,rc->dntc", arriving, jnp.asarray(placing), precision=lax.Precision.HIGHEST
    )
    diffuse_here = diffusivity[None, None]
    return wet_mask[:, None] * ((1.0 - 5.0 * diffuse_here) * weighted + interior + returned)


PADDED = 1024
SIDE_LANES = 32
PLANE = 4
HALVES = 2
MESH = pl.DeviceIdType.MESH


def strip_selector():
    chosen = np.zeros((PADDED + 128, 256), np.float32)
    for j in range(EDGE):
        for side, lane in enumerate([PADDED - EDGE + j, EDGE * EDGE + j, EDGE * j, EDGE * j + EDGE - 1]):
            chosen[lane, SIDE_LANES * side + j] = 1.0
            chosen[lane, 128 + SIDE_LANES * side + EDGE - 1 - j] = 1.0
    for corner, cell in enumerate([0, EDGE - 1, (EDGE - 1) * EDGE, EDGE * EDGE - 1]):
        chosen[PADDED + cell % 128, SIDE_LANES * corner + EDGE] = 1.0
    return jnp.asarray(chosen, jnp.bfloat16)


def strip_placer():
    placing = np.zeros((128, PADDED), np.float32)
    for j in range(EDGE):
        for side, cell in enumerate([j, (EDGE - 1) * EDGE + j, EDGE * j, EDGE * j + EDGE - 1]):
            placing[SIDE_LANES * side + j, cell] = 1.0
    for corner, cell in enumerate([0, EDGE - 1, (EDGE - 1) * EDGE, EDGE * EDGE - 1]):
        placing[SIDE_LANES * corner + EDGE, cell] = 1.0
    return jnp.asarray(placing, jnp.bfloat16)


def split_dot(left, right):
    high = left.astype(jnp.bfloat16)
    low = (left - high.astype(jnp.float32)).astype(jnp.bfloat16)
    return jnp.dot(high, right, preferred_element_type=jnp.float32) + jnp.dot(
        low, right, preferred_element_type=jnp.float32
    )


def four_times(pair):
    return jnp.concatenate([pair, pair, pair, pair], axis=0)


def widen(rows):
    return jnp.concatenate(
        [rows, jnp.zeros((rows.shape[0], PADDED - rows.shape[1]), rows.dtype)], axis=1
    )


def solve_kernel(
    code_hbm, cot_hbm, cx_hbm, cy_hbm, dif_hbm, vd_hbm, lc_hbm, sel_hbm,
    base_ref, strips_ref, factor_ref, partial_ref, edge_ref,
    code_ref, cot_ref, cx_ref, cy_ref, dif_ref, vd_ref, lc_ref, sel_ref, sems,
):
    levels = cot_ref.shape[0]
    cells = cot_ref.shape[3]
    pairs = [
        (lc_hbm, lc_ref),
        (vd_hbm, vd_ref),
        (cot_hbm, cot_ref),
        (dif_hbm, dif_ref),
        (cx_hbm, cx_ref),
        (cy_hbm, cy_ref),
        (code_hbm, code_ref),
        (sel_hbm, sel_ref),
    ]
    copies = [
        pltpu.make_async_copy(source, target, sems.at[i])
        for i, (source, target) in enumerate(pairs)
    ]
    for copy in copies:
        copy.start()
    for copy in copies[:3]:
        copy.wait()
    depth = four_times(lc_ref[...])

    def coupling(k):
        if k == 0 or k == levels:
            return jnp.zeros((8, cells), jnp.float32)
        return jnp.where(k < depth, four_times(vd_ref[k]), 0.0)

    factor = jnp.zeros((8, cells), jnp.float32)
    partial_value = jnp.zeros((8, cells), jnp.float32)
    upper = coupling(0)
    for k in range(levels):
        lower = coupling(k + 1)
        source = jnp.concatenate([cot_ref[k, n] for n in range(4)], axis=0)
        inverse = 1.0 / ((1.0 + upper + lower) + upper * factor)
        factor = -lower * inverse
        partial_value = (source + upper * partial_value) * inverse
        factor_ref[k] = factor
        partial_ref[k] = partial_value
        upper = lower

    lane = lax.broadcasted_iota(jnp.int32, (8, PADDED), 1)
    row_lane = jnp.where(lane >= PADDED - EDGE, lane - (PADDED - EDGE), lane)
    column = lax.rem(row_lane, EDGE)
    first = column == 0
    last = column == EDGE - 1
    inside = lane < cells
    short = lax.broadcasted_iota(jnp.int32, (8, 128), 1)
    corner_0 = (short == 0) | (short == EDGE - 1)
    corner_6 = short == ((EDGE - 1) * EDGE) % 128
    corner_7 = short == (EDGE * EDGE - 1) % 128
    for copy in copies[3:6]:
        copy.wait()
    diffuse = widen(four_times(dif_ref[...]))
    quarter = 0.25 * diffuse
    centre = 1.0 - 5.0 * diffuse
    wide_depth = widen(depth)
    solved = jnp.zeros((8, cells), jnp.float32)
    for k in reversed(range(levels)):
        solved = partial_ref[k] - factor_ref[k] * solved
        u = widen(jnp.where(k < depth, solved, 0.0))
        half_x = 0.5 * widen(four_times(cx_ref[k]))
        half_y = 0.5 * widen(four_times(cy_ref[k]))
        diagonal = quarter * u
        both = pltpu.roll(diagonal, EDGE, 1) + pltpu.roll(diagonal, PADDED - EDGE, 1)
        west = both + (diffuse + half_x) * u
        east = both + (diffuse - half_x) * u
        spread = pltpu.roll((diffuse + half_y) * u, PADDED - EDGE, 1)
        spread = spread + pltpu.roll((diffuse - half_y) * u, EDGE, 1)
        spread = spread + pltpu.roll(jnp.where(first, 0.0, west), PADDED - 1, 1)
        spread = spread + pltpu.roll(jnp.where(last, 0.0, east), 1, 1)
        base_ref[k] = jnp.where(k < wide_depth, centre * u + spread, 0.0)
        edge_ref[8 * k : 8 * k + 8, :PADDED] = jnp.where(
            inside, jnp.where(first, west, east), spread
        )
        edge_ref[8 * k : 8 * k + 8, PADDED:] = (
            jnp.where(corner_0, diagonal[:, 0:128], 0.0)
            + jnp.where(corner_6, diagonal[:, 768:896], 0.0)
            + jnp.where(corner_7, diagonal[:, 896:1024], 0.0)
        )
    for copy in copies[6:]:
        copy.wait()
    both_ways = split_dot(edge_ref[...], sel_ref[...])
    parity = lax.rem(lax.broadcasted_iota(jnp.int32, (8, 128), 0), 2)
    code = jnp.zeros((8, 128), jnp.int32)
    for i in range(2):
        for side in range(4):
            code = jnp.where((parity == i) & (short // SIDE_LANES == side), code_ref[i, side], code)
    flipped = (code >= 4) & (lax.rem(short, SIDE_LANES) < EDGE)
    for k in range(levels):
        rows = both_ways[8 * k : 8 * k + 8]
        strips_ref[k] = jnp.where(flipped, rows[:, 128:], rows[:, :128])


def send_kernel(count, strips_ref, near_ref, own_sem, send_sem, recv_sem):
    chips = count // 2
    me = lax.axis_index("tile")
    chip = me // 2
    core = lax.rem(me, 2)
    place = lax.rem(chip, PLANE)

    def at(steps):
        return 2 * lax.rem(chip + steps + chips, chips) + core

    partner = me + 1 - 2 * core
    wraps = [(place + j) // PLANE for j in range(PLANE)]
    beside = [at(j - PLANE * wraps[j]) for j in range(PLANE)]
    above, below = at(PLANE), at(-PLANE)
    barrier = pltpu.get_barrier_semaphore()
    peers = [partner, above, below] + beside[1:]
    for peer in peers:
        pl.semaphore_signal(barrier, inc=1, device_id={"tile": peer}, device_id_type=MESH)
    own = pltpu.make_async_copy(strips_ref, near_ref.at[PLANE, core], own_sem)
    own.start()
    pl.semaphore_wait(barrier, len(peers))
    copies = []
    size = strips_ref.shape[0] // HALVES

    def part(spot, side, half):
        return near_ref.at[spot, side, half * size : (half + 1) * size]

    def mine(half):
        return strips_ref.at[half * size : (half + 1) * size]

    def send(source, spot, half, to):
        copy = pltpu.make_async_remote_copy(
            src_ref=source,
            dst_ref=part(spot, core, half),
            send_sem=send_sem.at[len(copies)],
            recv_sem=recv_sem.at[spot, core, half],
            device_id={"tile": to},
            device_id_type=MESH,
        )
        copy.start()
        copies.append(copy)

    def arrived(spot, side, half):
        pltpu.make_async_remote_copy(
            src_ref=mine(half),
            dst_ref=part(spot, side, half),
            send_sem=own_sem,
            recv_sem=recv_sem.at[spot, side, half],
            device_id={"tile": partner},
            device_id_type=MESH,
        ).wait_recv()

    def share(spot, half):
        send(part(spot, core, half), spot, half, partner)

    for half in range(HALVES):
        send(mine(half), 0, half, above)
        send(mine(half), 2 * PLANE, half, below)
    for half in range(HALVES):
        for j in range(1, PLANE):
            send(mine(half), PLANE - j + PLANE * wraps[j], half, beside[j])
        send(mine(half), PLANE, half, partner)
    for half in range(HALVES):
        arrived(0, core, half)
        arrived(2 * PLANE, core, half)
        for j in range(1, PLANE):
            source = part(2 * PLANE - 2 * PLANE * wraps[j], core, half)
            send(source, 2 * PLANE - PLANE * wraps[j] - j, half, beside[j])
        share(0, half)
        share(2 * PLANE, half)
    for half in range(HALVES):
        for j in range(1, PLANE):
            spot = PLANE + j - PLANE * wraps[j]
            arrived(spot, core, half)
            share(spot, half)
    for half in range(HALVES):
        for j in range(1, PLANE):
            spot = j + PLANE * wraps[j]
            arrived(spot, core, half)
            share(spot, half)
    for half in range(HALVES):
        for spot in range(2 * PLANE + 1):
            arrived(spot, 1 - core, half)
    own.wait()
    for copy in copies:
        copy.wait_send()


def place_kernel(
    count, et_ref, ec_ref, ct_ref, cc_ref, near_ref, base_ref, lc_ref, place_ref,
    out_ref, arriving_ref,
):
    levels = base_ref.shape[0]
    cells = out_ref.shape[3]
    me = lax.axis_index("tile")
    lane = lax.broadcasted_iota(jnp.int32, (8, 128), 1)
    parity = lax.rem(lax.broadcasted_iota(jnp.int32, (8, 128), 0), 2)
    group = lane // SIDE_LANES
    spot = lax.rem(lane, SIDE_LANES)
    total = jnp.zeros((levels, 8, 128), jnp.float32)
    for i in range(2):
        for tiles_ref, codes_ref, wanted in (
            (et_ref, ec_ref, spot < EDGE),
            (ct_ref, cc_ref, spot == EDGE),
        ):
            for side in range(4):
                tile = tiles_ref[i, side]
                there = jnp.maximum(tile, 0)
                slot = lax.rem(there // 4 - me // 2 + PLANE + count // 2, count // 2)
                slot = jnp.where(tile < 0, 0, slot)
                values = near_ref[slot, lax.rem(there // 2, 2)]
                values = jnp.where(
                    lax.rem(there, 2) == i, values, pltpu.roll(values, 1 if i == 1 else 7, 1)
                )
                shift = lax.rem(SIDE_LANES * (side - lax.rem(codes_ref[i, side], 4)) + 128, 128)
                values = pltpu.roll(values, shift, 2)
                chosen = wanted & (group == side) & (parity == i) & (tile >= 0)
                total = jnp.where(chosen[None], values, total)
    for k in range(levels):
        arriving_ref[8 * k : 8 * k + 8] = total[k]
    returned = split_dot(arriving_ref[...], place_ref[...])
    depth = four_times(lc_ref[...])
    for k in range(levels):
        result = base_ref[k][:, :cells] + jnp.where(
            k < depth, returned[8 * k : 8 * k + 8, :cells], 0.0
        )
        for n in range(4):
            out_ref[k, n] = result[2 * n : 2 * n + 2]


def shards_fast(
    cotangent,
    courant_x,
    courant_y,
    diffusivity,
    vert_diff,
    level_count,
    edge_tile,
    edge_code,
    corner_tile,
    corner_code,
):
    levels, tracers, tiles_here, cells = cotangent.shape
    count = lax.axis_size("tile")
    vmem = pl.BlockSpec(memory_space=pltpu.VMEM)
    smem = pl.BlockSpec(memory_space=pltpu.SMEM)
    hbm = pl.BlockSpec(memory_space=pltpu.HBM)
    base, strips = pl.pallas_call(
        solve_kernel,
        name="solve",
        out_shape=(
            jax.ShapeDtypeStruct((levels, 8, PADDED), jnp.float32),
            jax.ShapeDtypeStruct((levels, 8, 128), jnp.float32),
        ),
        in_specs=[hbm] * 8,
        out_specs=(vmem, vmem),
        scratch_shapes=[
            pltpu.VMEM((levels, 8, cells), jnp.float32),
            pltpu.VMEM((levels, 8, cells), jnp.float32),
            pltpu.VMEM((8 * levels, PADDED + 128), jnp.float32),
            pltpu.SMEM(edge_code.shape, jnp.int32),
            pltpu.VMEM(cotangent.shape, jnp.float32),
            pltpu.VMEM(courant_x.shape, jnp.float32),
            pltpu.VMEM(courant_y.shape, jnp.float32),
            pltpu.VMEM(diffusivity.shape, jnp.float32),
            pltpu.VMEM(vert_diff.shape, jnp.float32),
            pltpu.VMEM(level_count.shape, jnp.int32),
            pltpu.VMEM((PADDED + 128, 256), jnp.bfloat16),
            pltpu.SemaphoreType.DMA((8,)),
        ],
        compiler_params=pltpu.CompilerParams(vmem_limit_bytes=62 << 20),
    )(edge_code, cotangent, courant_x, courant_y, diffusivity, vert_diff, level_count, strip_selector())
    near = pl.pallas_call(
        functools.partial(send_kernel, count),
        name="send",
        out_shape=jax.ShapeDtypeStruct((2 * PLANE + 1, 2, levels, 8, 128), jnp.float32),
        in_specs=[hbm],
        out_specs=hbm,
        scratch_shapes=[
            pltpu.SemaphoreType.DMA,
            pltpu.SemaphoreType.DMA((HALVES * (4 * PLANE + 1),)),
            pltpu.SemaphoreType.DMA((2 * PLANE + 1, 2, HALVES)),
        ],
        compiler_params=pltpu.CompilerParams(collective_id=0, has_side_effects=True),
    )(strips)
    return pl.pallas_call(
        functools.partial(place_kernel, count),
        name="place",
        out_shape=jax.ShapeDtypeStruct(cotangent.shape, jnp.float32),
        in_specs=[smem] * 4 + [vmem] * 4,
        out_specs=vmem,
        scratch_shapes=[pltpu.VMEM((8 * levels, 128), jnp.float32)],
        compiler_params=pltpu.CompilerParams(vmem_limit_bytes=40 << 20),
    )(edge_tile, edge_code, corner_tile, corner_code, near, base, level_count, strip_placer())


def solution(mesh):
    placed = (
        P("lev", None, "tile", None),
        P("lev", "tile", None),
        P("lev", "tile", None),
        P("tile", None),
        P("lev", "tile", None),
        P("tile", None),
        P("tile", None),
        P("tile", None),
        P("tile", None),
        P("tile", None),
    )
    fast = mesh.shape["lev"] == 1 and mesh.shape["tile"] % 8 == 0 and mesh.shape["tile"] > 2 * BAND
    return jax.shard_map(
        shards_fast if fast else shards, mesh=mesh, in_specs=placed, out_specs=P("lev", None, "tile", None), check_vma=False
    )
```

```python
import functools

import jax
import jax.numpy as jnp
import numpy as np
from jax import lax
from jax.experimental import pallas as pl
from jax.experimental.pallas import tpu as pltpu
from jax.sharding import PartitionSpec as P

EDGE = 30
BAND = 8


stencil_offsets = [(0, -1), (0, 1), (-1, 0), (1, 0), (-1, -1), (-1, 1), (1, -1), (1, 1)]


def from_behind(value, axis, steps):
    count = lax.axis_size(axis)
    initial, last = (max(0, -steps), min(count, count - steps))
    return lax.ppermute(value, axis, [(source, source + steps) for source in range(initial, last)])


def shifted_2(value, axis, by):
    devices = lax.axis_size(axis)
    return lax.ppermute(value, axis, [(i, (i + by) % devices) for i in range(devices)])


def stencil_weights(diffuse, flow_x, flow_y):
    return [
        diffuse + 0.5 * flow_x,
        diffuse - 0.5 * flow_x,
        diffuse + 0.5 * flow_y,
        diffuse - 0.5 * flow_y,
        0.25 * diffuse,
        0.25 * diffuse,
        0.25 * diffuse,
        0.25 * diffuse,
    ]


def eliminate(right_side, coupling_up, coupling_down, initial):

    def advance(state, inputs):
        factor, partial_value = state
        source, upper_term, lower_term = inputs
        divisor = 1.0 + upper_term + lower_term + upper_term * factor
        factor_new = -lower_term / divisor
        partial_new = (source + upper_term * partial_value) / divisor
        return ((factor_new, partial_new), (factor_new, partial_new))

    final_state, outputs = lax.scan(advance, initial, (right_side, coupling_up, coupling_down))
    return outputs


def substitute(factors, partials, below_field):

    def backward(state, inputs):
        factor, partial_value = inputs
        column_value = partial_value - factor * state
        return (column_value, column_value)

    final_state, fields = lax.scan(backward, below_field, (factors, partials), reverse=True)
    return fields


def cycle_tables():
    padded_edge = EDGE + 2
    cycle_spots = []
    cell_spots = []
    for border in range(4):
        for position in range(EDGE):
            if border == 0:
                cycle_spots.append(position + 1)
                cell_spots.append(position)
            elif border == 1:
                cycle_spots.append((padded_edge - 1) * padded_edge + position + 1)
                cell_spots.append((EDGE - 1) * EDGE + position)
            elif border == 2:
                cycle_spots.append((position + 1) * padded_edge)
                cell_spots.append(position * EDGE)
            else:
                cycle_spots.append((position + 1) * padded_edge + padded_edge - 1)
                cell_spots.append(position * EDGE + EDGE - 1)
    cycle_spots += [
        0,
        padded_edge - 1,
        (padded_edge - 1) * padded_edge,
        padded_edge * padded_edge - 1,
    ]
    cell_spots += [0, EDGE - 1, (EDGE - 1) * EDGE, EDGE * EDGE - 1]
    placing = np.zeros((len(cycle_spots), EDGE * EDGE), np.float32)
    placing[np.arange(len(cycle_spots)), np.array(cell_spots)] = 1.0
    return (np.array(cycle_spots, np.int32), placing)


def embed(field):
    leading = field.shape[:-1]
    square = field.reshape(leading + (EDGE, EDGE))
    padded = jnp.pad(square, [(0, 0)] * len(leading) + [(1, 1), (1, 1)])
    return padded.reshape(leading + ((EDGE + 2) * (EDGE + 2),))


def shards(
    cotangent,
    courant_x,
    courant_y,
    diffusivity,
    vert_diff,
    level_count,
    edge_tile,
    edge_code,
    corner_tile,
    corner_code,
):
    levels_here = cotangent.shape[0]
    tracers = cotangent.shape[1]
    tiles_here = cotangent.shape[2]
    cells = cotangent.shape[3]
    padded_edge = EDGE + 2
    cycle_size = 4 * EDGE + 4
    lev_count = lax.axis_size("lev")
    depth_index = (
        lax.axis_index("lev") * levels_here
        + jnp.arange(levels_here, dtype=jnp.int32)[:, None, None]
    )
    wet_mask = (depth_index < level_count[None]).astype(jnp.float32)
    coupling = jnp.where(depth_index == 0, jnp.float32(0.0), vert_diff * wet_mask)
    deeper = from_behind(coupling[0], "lev", -1)
    coupling_down = jnp.concatenate([coupling[1:], deeper[None]], axis=0)[:, None]
    coupling_up = coupling[:, None]
    initial = (
        jnp.zeros((1, tiles_here, cells), jnp.float32),
        jnp.zeros((tracers, tiles_here, cells), jnp.float32),
    )
    for sweep_index in range(lev_count - 1):
        factors, partials = eliminate(cotangent, coupling_up, coupling_down, initial)
        initial = from_behind((factors[-1], partials[-1]), "lev", 1)
    factors, partials = eliminate(cotangent, coupling_up, coupling_down, initial)
    below_field = jnp.zeros((tracers, tiles_here, cells), jnp.float32)
    for sweep_index in range(lev_count - 1):
        fields = substitute(factors, partials, below_field)
        below_field = from_behind(fields[0], "lev", -1)
    solved = substitute(factors, partials, below_field)
    weighted = solved * wet_mask[:, None]
    weighted_ext = embed(weighted)
    diffuse_ext = embed(diffusivity)[None, None]
    flow_x_ext = embed(courant_x)[:, None]
    flow_y_ext = embed(courant_y)[:, None]
    weights = stencil_weights(diffuse_ext, flow_x_ext, flow_y_ext)
    leading = weighted_ext.shape[:-1]
    spread = jnp.zeros_like(weighted_ext)
    for (shift_row, shift_col), weight in zip(stencil_offsets, weights):
        contribution = weight * weighted_ext
        offset = shift_row * padded_edge + shift_col
        if offset > 0:
            shifted = jnp.concatenate(
                [jnp.zeros(leading + (offset,), jnp.float32), contribution[..., :-offset]], axis=-1
            )
        else:
            shifted = jnp.concatenate(
                [contribution[..., -offset:], jnp.zeros(leading + (-offset,), jnp.float32)], axis=-1
            )
        spread = spread + shifted
    cycle_spots, placing = cycle_tables()
    outgoing = jnp.take(spread, jnp.asarray(cycle_spots), axis=3)
    interior = spread.reshape(leading + (padded_edge, padded_edge))[..., 1:-1, 1:-1].reshape(
        solved.shape
    )
    partners = jnp.concatenate([edge_tile, corner_tile], axis=1)

    def collect(gathered_sum, portion, first_tile):
        tile_span = portion.shape[2]
        onehot = (
            partners[:, :, None]
            == first_tile + jnp.arange(tile_span, dtype=jnp.int32)[None, None, :]
        ).astype(jnp.float32)
        return gathered_sum + jnp.einsum(
            "tkw,dnwr->dntkr", onehot, portion, precision=lax.Precision.HIGHEST
        )

    tile_count = lax.axis_size("tile")
    own_index = lax.axis_index("tile")
    reach = (2 * BAND + tiles_here - 1) // tiles_here
    fetched = collect(
        jnp.zeros((levels_here, tracers, tiles_here, 8, cycle_size), jnp.float32),
        outgoing,
        own_index * tiles_here,
    )
    for distance in range(-reach, reach + 1):
        if distance != 0:
            portion = shifted_2(outgoing, "tile", distance)
            source = (own_index - distance) % tile_count
            fetched = collect(fetched, portion, source * tiles_here)
    side_values = fetched[:, :, :, :4, : 4 * EDGE].reshape(
        levels_here, tracers, tiles_here, 4, 4, EDGE
    )
    side_choice = (
        (edge_code % 4)[:, :, None] == jnp.arange(4, dtype=jnp.int32)[None, None, :]
    ).astype(jnp.float32)
    strips = jnp.sum(side_values * side_choice[None, None, :, :, :, None], axis=4)
    strips = jnp.where((edge_code >= 4)[None, None, :, :, None], strips[..., ::-1], strips)
    corner_values = fetched[:, :, :, 4:, 4 * EDGE :]
    corner_choice = (
        corner_code[:, :, None] == jnp.arange(4, dtype=jnp.int32)[None, None, :]
    ).astype(jnp.float32)
    corner_picked = jnp.sum(corner_values * corner_choice[None, None], axis=4)
    arriving = jnp.concatenate(
        [strips.reshape(levels_here, tracers, tiles_here, 4 * EDGE), corner_picked], axis=3
    )
    returned = jnp.einsum(
        "dntr,rc->dntc", arriving, jnp.asarray(placing), precision=lax.Precision.HIGHEST
    )
    diffuse_here = diffusivity[None, None]
    return wet_mask[:, None] * ((1.0 - 5.0 * diffuse_here) * weighted + interior + returned)


PADDED = 1024
SIDE_LANES = 32
PLANE = 4
MESH = pl.DeviceIdType.MESH


def strip_selector():
    chosen = np.zeros((PADDED + 128, 256), np.float32)
    for j in range(EDGE):
        for side, lane in enumerate([PADDED - EDGE + j, EDGE * EDGE + j, EDGE * j, EDGE * j + EDGE - 1]):
            chosen[lane, SIDE_LANES * side + j] = 1.0
            chosen[lane, 128 + SIDE_LANES * side + EDGE - 1 - j] = 1.0
    for corner, cell in enumerate([0, EDGE - 1, (EDGE - 1) * EDGE, EDGE * EDGE - 1]):
        chosen[PADDED + cell % 128, SIDE_LANES * corner + EDGE] = 1.0
    return jnp.asarray(chosen, jnp.bfloat16)


def strip_placer():
    placing = np.zeros((128, PADDED), np.float32)
    for j in range(EDGE):
        for side, cell in enumerate([j, (EDGE - 1) * EDGE + j, EDGE * j, EDGE * j + EDGE - 1]):
            placing[SIDE_LANES * side + j, cell] = 1.0
    for corner, cell in enumerate([0, EDGE - 1, (EDGE - 1) * EDGE, EDGE * EDGE - 1]):
        placing[SIDE_LANES * corner + EDGE, cell] = 1.0
    return jnp.asarray(placing, jnp.bfloat16)


def split_dot(left, right):
    high = left.astype(jnp.bfloat16)
    low = (left - high.astype(jnp.float32)).astype(jnp.bfloat16)
    return jnp.dot(high, right, preferred_element_type=jnp.float32) + jnp.dot(
        low, right, preferred_element_type=jnp.float32
    )


def four_times(pair):
    return jnp.concatenate([pair, pair, pair, pair], axis=0)


def widen(rows):
    return jnp.concatenate(
        [rows, jnp.zeros((rows.shape[0], PADDED - rows.shape[1]), rows.dtype)], axis=1
    )


def solve_kernel(
    code_hbm, cot_hbm, cx_hbm, cy_hbm, dif_hbm, vd_hbm, lc_hbm, sel_hbm,
    base_ref, strips_ref, factor_ref, partial_ref, edge_ref,
    code_ref, cot_ref, cx_ref, cy_ref, dif_ref, vd_ref, lc_ref, sel_ref, sems,
):
    levels = cot_ref.shape[0]
    cells = cot_ref.shape[3]
    pairs = [
        (lc_hbm, lc_ref),
        (vd_hbm, vd_ref),
        (cot_hbm, cot_ref),
        (dif_hbm, dif_ref),
        (cx_hbm, cx_ref),
        (cy_hbm, cy_ref),
        (code_hbm, code_ref),
        (sel_hbm, sel_ref),
    ]
    copies = [
        pltpu.make_async_copy(source, target, sems.at[i])
        for i, (source, target) in enumerate(pairs)
    ]
    for copy in copies:
        copy.start()
    for copy in copies[:3]:
        copy.wait()
    depth = four_times(lc_ref[...])

    def coupling(k):
        if k == 0 or k == levels:
            return jnp.zeros((8, cells), jnp.float32)
        return jnp.where(k < depth, four_times(vd_ref[k]), 0.0)

    factor = jnp.zeros((8, cells), jnp.float32)
    partial_value = jnp.zeros((8, cells), jnp.float32)
    upper = coupling(0)
    for k in range(levels):
        lower = coupling(k + 1)
        source = jnp.concatenate([cot_ref[k, n] for n in range(4)], axis=0)
        inverse = 1.0 / ((1.0 + upper + lower) + upper * factor)
        factor = -lower * inverse
        partial_value = (source + upper * partial_value) * inverse
        factor_ref[k] = factor
        partial_ref[k] = partial_value
        upper = lower

    lane = lax.broadcasted_iota(jnp.int32, (8, PADDED), 1)
    row_lane = jnp.where(lane >= PADDED - EDGE, lane - (PADDED - EDGE), lane)
    column = lax.rem(row_lane, EDGE)
    first = column == 0
    last = column == EDGE - 1
    inside = lane < cells
    short = lax.broadcasted_iota(jnp.int32, (8, 128), 1)
    corner_0 = (short == 0) | (short == EDGE - 1)
    corner_6 = short == ((EDGE - 1) * EDGE) % 128
    corner_7 = short == (EDGE * EDGE - 1) % 128
    for copy in copies[3:6]:
        copy.wait()
    diffuse = widen(four_times(dif_ref[...]))
    quarter = 0.25 * diffuse
    centre = 1.0 - 5.0 * diffuse
    wide_depth = widen(depth)
    solved = jnp.zeros((8, cells), jnp.float32)
    for k in reversed(range(levels)):
        solved = partial_ref[k] - factor_ref[k] * solved
        u = widen(jnp.where(k < depth, solved, 0.0))
        half_x = 0.5 * widen(four_times(cx_ref[k]))
        half_y = 0.5 * widen(four_times(cy_ref[k]))
        diagonal = quarter * u
        both = pltpu.roll(diagonal, EDGE, 1) + pltpu.roll(diagonal, PADDED - EDGE, 1)
        west = both + (diffuse + half_x) * u
        east = both + (diffuse - half_x) * u
        spread = pltpu.roll((diffuse + half_y) * u, PADDED - EDGE, 1)
        spread = spread + pltpu.roll((diffuse - half_y) * u, EDGE, 1)
        spread = spread + pltpu.roll(jnp.where(first, 0.0, west), PADDED - 1, 1)
        spread = spread + pltpu.roll(jnp.where(last, 0.0, east), 1, 1)
        base_ref[k] = jnp.where(k < wide_depth, centre * u + spread, 0.0)
        edge_ref[8 * k : 8 * k + 8, :PADDED] = jnp.where(
            inside, jnp.where(first, west, east), spread
        )
        edge_ref[8 * k : 8 * k + 8, PADDED:] = (
            jnp.where(corner_0, diagonal[:, 0:128], 0.0)
            + jnp.where(corner_6, diagonal[:, 768:896], 0.0)
            + jnp.where(corner_7, diagonal[:, 896:1024], 0.0)
        )
    for copy in copies[6:]:
        copy.wait()
    both_ways = split_dot(edge_ref[...], sel_ref[...])
    parity = lax.rem(lax.broadcasted_iota(jnp.int32, (8, 128), 0), 2)
    code = jnp.zeros((8, 128), jnp.int32)
    for i in range(2):
        for side in range(4):
            code = jnp.where((parity == i) & (short // SIDE_LANES == side), code_ref[i, side], code)
    flipped = (code >= 4) & (lax.rem(short, SIDE_LANES) < EDGE)
    for k in range(levels):
        rows = both_ways[8 * k : 8 * k + 8]
        strips_ref[k] = jnp.where(flipped, rows[:, 128:], rows[:, :128])


def send_kernel(count, strips_ref, near_ref, own_sem, send_sem, recv_sem):
    chips = count // 2
    me = lax.axis_index("tile")
    chip = me // 2
    core = lax.rem(me, 2)
    place = lax.rem(chip, PLANE)

    def at(steps):
        return 2 * lax.rem(chip + steps + chips, chips) + core

    partner = me + 1 - 2 * core
    dx = 1 - 2 * lax.rem(place, 2)
    dy = 2 - 4 * (place // 2)
    along_x, along_y = at(dx), at(dy)
    above, below = at(PLANE), at(-PLANE)
    barrier = pltpu.get_barrier_semaphore()
    peers = [partner, above, below, along_x, along_y]
    for peer in peers:
        pl.semaphore_signal(barrier, inc=1, device_id={"tile": peer}, device_id_type=MESH)
    own = pltpu.make_async_copy(strips_ref, near_ref.at[PLANE, core], own_sem)
    own.start()
    pl.semaphore_wait(barrier, len(peers))
    copies = []

    def send(source, spot, to):
        copy = pltpu.make_async_remote_copy(
            src_ref=source,
            dst_ref=near_ref.at[spot, core],
            send_sem=send_sem.at[len(copies)],
            recv_sem=recv_sem.at[spot, core],
            device_id={"tile": to},
            device_id_type=MESH,
        )
        copy.start()
        copies.append(copy)

    def arrived(spot, side):
        pltpu.make_async_remote_copy(
            src_ref=strips_ref,
            dst_ref=near_ref.at[spot, side],
            send_sem=own_sem,
            recv_sem=recv_sem.at[spot, side],
            device_id={"tile": partner},
            device_id_type=MESH,
        ).wait_recv()

    def share(spot):
        send(near_ref.at[spot, core], spot, partner)

    def relay(spot, there, to):
        send(near_ref.at[spot, core], there, to)

    send(strips_ref, 0, above)
    send(strips_ref, 2 * PLANE, below)
    send(strips_ref, PLANE - dx, along_x)
    send(strips_ref, PLANE - dy, along_y)
    send(strips_ref, PLANE, partner)
    arrived(PLANE + dx, core)
    relay(PLANE + dx, PLANE + dx - dy, along_y)
    share(PLANE + dx)
    arrived(0, core)
    arrived(2 * PLANE, core)
    relay(PLANE + 2 * dy, PLANE + dy, along_y)
    relay(PLANE + 4 * dx, PLANE + 3 * dx, along_x)
    share(0)
    share(2 * PLANE)
    arrived(PLANE - dy, core)
    relay(PLANE - dy, PLANE - dy - dx, along_x)
    share(PLANE - dy)
    for spot in (PLANE + dy, PLANE + dx + dy, PLANE - 3 * dx, PLANE - dy + dx):
        arrived(spot, core)
        share(spot)
    for spot in range(2 * PLANE + 1):
        arrived(spot, 1 - core)
    own.wait()
    for copy in copies:
        copy.wait_send()


def place_kernel(
    count, et_ref, ec_ref, ct_ref, cc_ref, near_ref, base_ref, lc_ref, place_ref,
    out_ref, arriving_ref,
):
    levels = base_ref.shape[0]
    cells = out_ref.shape[3]
    me = lax.axis_index("tile")
    lane = lax.broadcasted_iota(jnp.int32, (8, 128), 1)
    parity = lax.rem(lax.broadcasted_iota(jnp.int32, (8, 128), 0), 2)
    group = lane // SIDE_LANES
    spot = lax.rem(lane, SIDE_LANES)
    total = jnp.zeros((levels, 8, 128), jnp.float32)
    for i in range(2):
        for tiles_ref, codes_ref, wanted in (
            (et_ref, ec_ref, spot < EDGE),
            (ct_ref, cc_ref, spot == EDGE),
        ):
            for side in range(4):
                tile = tiles_ref[i, side]
                there = jnp.maximum(tile, 0)
                slot = lax.rem(there // 4 - me // 2 + PLANE + count // 2, count // 2)
                slot = jnp.where(tile < 0, 0, slot)
                values = near_ref[slot, lax.rem(there // 2, 2)]
                values = jnp.where(
                    lax.rem(there, 2) == i, values, pltpu.roll(values, 1 if i == 1 else 7, 1)
                )
                shift = lax.rem(SIDE_LANES * (side - lax.rem(codes_ref[i, side], 4)) + 128, 128)
                values = pltpu.roll(values, shift, 2)
                chosen = wanted & (group == side) & (parity == i) & (tile >= 0)
                total = jnp.where(chosen[None], values, total)
    for k in range(levels):
        arriving_ref[8 * k : 8 * k + 8] = total[k]
    returned = split_dot(arriving_ref[...], place_ref[...])
    depth = four_times(lc_ref[...])
    for k in range(levels):
        result = base_ref[k][:, :cells] + jnp.where(
            k < depth, returned[8 * k : 8 * k + 8, :cells], 0.0
        )
        for n in range(4):
            out_ref[k, n] = result[2 * n : 2 * n + 2]


def shards_fast(
    cotangent,
    courant_x,
    courant_y,
    diffusivity,
    vert_diff,
    level_count,
    edge_tile,
    edge_code,
    corner_tile,
    corner_code,
):
    levels, tracers, tiles_here, cells = cotangent.shape
    count = lax.axis_size("tile")
    vmem = pl.BlockSpec(memory_space=pltpu.VMEM)
    smem = pl.BlockSpec(memory_space=pltpu.SMEM)
    hbm = pl.BlockSpec(memory_space=pltpu.HBM)
    base, strips = pl.pallas_call(
        solve_kernel,
        name="solve",
        out_shape=(
            jax.ShapeDtypeStruct((levels, 8, PADDED), jnp.float32),
            jax.ShapeDtypeStruct((levels, 8, 128), jnp.float32),
        ),
        in_specs=[hbm] * 8,
        out_specs=(vmem, vmem),
        scratch_shapes=[
            pltpu.VMEM((levels, 8, cells), jnp.float32),
            pltpu.VMEM((levels, 8, cells), jnp.float32),
            pltpu.VMEM((8 * levels, PADDED + 128), jnp.float32),
            pltpu.SMEM(edge_code.shape, jnp.int32),
            pltpu.VMEM(cotangent.shape, jnp.float32),
            pltpu.VMEM(courant_x.shape, jnp.float32),
            pltpu.VMEM(courant_y.shape, jnp.float32),
            pltpu.VMEM(diffusivity.shape, jnp.float32),
            pltpu.VMEM(vert_diff.shape, jnp.float32),
            pltpu.VMEM(level_count.shape, jnp.int32),
            pltpu.VMEM((PADDED + 128, 256), jnp.bfloat16),
            pltpu.SemaphoreType.DMA((8,)),
        ],
        compiler_params=pltpu.CompilerParams(vmem_limit_bytes=62 << 20),
    )(edge_code, cotangent, courant_x, courant_y, diffusivity, vert_diff, level_count, strip_selector())
    near = pl.pallas_call(
        functools.partial(send_kernel, count),
        name="send",
        out_shape=jax.ShapeDtypeStruct((2 * PLANE + 1, 2, levels, 8, 128), jnp.float32),
        in_specs=[hbm],
        out_specs=hbm,
        scratch_shapes=[
            pltpu.SemaphoreType.DMA,
            pltpu.SemaphoreType.DMA((4 * PLANE + 1,)),
            pltpu.SemaphoreType.DMA((2 * PLANE + 1, 2)),
        ],
        compiler_params=pltpu.CompilerParams(collective_id=0, has_side_effects=True),
    )(strips)
    return pl.pallas_call(
        functools.partial(place_kernel, count),
        name="place",
        out_shape=jax.ShapeDtypeStruct(cotangent.shape, jnp.float32),
        in_specs=[smem] * 4 + [vmem] * 4,
        out_specs=vmem,
        scratch_shapes=[pltpu.VMEM((8 * levels, 128), jnp.float32)],
        compiler_params=pltpu.CompilerParams(vmem_limit_bytes=40 << 20),
    )(edge_tile, edge_code, corner_tile, corner_code, near, base, level_count, strip_placer())


def solution(mesh):
    placed = (
        P("lev", None, "tile", None),
        P("lev", "tile", None),
        P("lev", "tile", None),
        P("tile", None),
        P("lev", "tile", None),
        P("tile", None),
        P("tile", None),
        P("tile", None),
        P("tile", None),
        P("tile", None),
    )
    fast = mesh.shape["lev"] == 1 and mesh.shape["tile"] % 8 == 0 and mesh.shape["tile"] > 2 * BAND
    return jax.shard_map(
        shards_fast if fast else shards, mesh=mesh, in_specs=placed, out_specs=P("lev", None, "tile", None), check_vma=False
    )
```

```python
import functools

import jax
import jax.numpy as jnp
import numpy as np
from jax import lax
from jax.experimental import pallas as pl
from jax.experimental.pallas import tpu as pltpu
from jax.sharding import PartitionSpec as P

EDGE = 30
BAND = 8


stencil_offsets = [(0, -1), (0, 1), (-1, 0), (1, 0), (-1, -1), (-1, 1), (1, -1), (1, 1)]


def from_behind(value, axis, steps):
    count = lax.axis_size(axis)
    initial, last = (max(0, -steps), min(count, count - steps))
    return lax.ppermute(value, axis, [(source, source + steps) for source in range(initial, last)])


def shifted_2(value, axis, by):
    devices = lax.axis_size(axis)
    return lax.ppermute(value, axis, [(i, (i + by) % devices) for i in range(devices)])


def stencil_weights(diffuse, flow_x, flow_y):
    return [
        diffuse + 0.5 * flow_x,
        diffuse - 0.5 * flow_x,
        diffuse + 0.5 * flow_y,
        diffuse - 0.5 * flow_y,
        0.25 * diffuse,
        0.25 * diffuse,
        0.25 * diffuse,
        0.25 * diffuse,
    ]


def eliminate(right_side, coupling_up, coupling_down, initial):

    def advance(state, inputs):
        factor, partial_value = state
        source, upper_term, lower_term = inputs
        divisor = 1.0 + upper_term + lower_term + upper_term * factor
        factor_new = -lower_term / divisor
        partial_new = (source + upper_term * partial_value) / divisor
        return ((factor_new, partial_new), (factor_new, partial_new))

    final_state, outputs = lax.scan(advance, initial, (right_side, coupling_up, coupling_down))
    return outputs


def substitute(factors, partials, below_field):

    def backward(state, inputs):
        factor, partial_value = inputs
        column_value = partial_value - factor * state
        return (column_value, column_value)

    final_state, fields = lax.scan(backward, below_field, (factors, partials), reverse=True)
    return fields


def cycle_tables():
    padded_edge = EDGE + 2
    cycle_spots = []
    cell_spots = []
    for border in range(4):
        for position in range(EDGE):
            if border == 0:
                cycle_spots.append(position + 1)
                cell_spots.append(position)
            elif border == 1:
                cycle_spots.append((padded_edge - 1) * padded_edge + position + 1)
                cell_spots.append((EDGE - 1) * EDGE + position)
            elif border == 2:
                cycle_spots.append((position + 1) * padded_edge)
                cell_spots.append(position * EDGE)
            else:
                cycle_spots.append((position + 1) * padded_edge + padded_edge - 1)
                cell_spots.append(position * EDGE + EDGE - 1)
    cycle_spots += [
        0,
        padded_edge - 1,
        (padded_edge - 1) * padded_edge,
        padded_edge * padded_edge - 1,
    ]
    cell_spots += [0, EDGE - 1, (EDGE - 1) * EDGE, EDGE * EDGE - 1]
    placing = np.zeros((len(cycle_spots), EDGE * EDGE), np.float32)
    placing[np.arange(len(cycle_spots)), np.array(cell_spots)] = 1.0
    return (np.array(cycle_spots, np.int32), placing)


def embed(field):
    leading = field.shape[:-1]
    square = field.reshape(leading + (EDGE, EDGE))
    padded = jnp.pad(square, [(0, 0)] * len(leading) + [(1, 1), (1, 1)])
    return padded.reshape(leading + ((EDGE + 2) * (EDGE + 2),))


def shards(
    cotangent,
    courant_x,
    courant_y,
    diffusivity,
    vert_diff,
    level_count,
    edge_tile,
    edge_code,
    corner_tile,
    corner_code,
):
    levels_here = cotangent.shape[0]
    tracers = cotangent.shape[1]
    tiles_here = cotangent.shape[2]
    cells = cotangent.shape[3]
    padded_edge = EDGE + 2
    cycle_size = 4 * EDGE + 4
    lev_count = lax.axis_size("lev")
    depth_index = (
        lax.axis_index("lev") * levels_here
        + jnp.arange(levels_here, dtype=jnp.int32)[:, None, None]
    )
    wet_mask = (depth_index < level_count[None]).astype(jnp.float32)
    coupling = jnp.where(depth_index == 0, jnp.float32(0.0), vert_diff * wet_mask)
    deeper = from_behind(coupling[0], "lev", -1)
    coupling_down = jnp.concatenate([coupling[1:], deeper[None]], axis=0)[:, None]
    coupling_up = coupling[:, None]
    initial = (
        jnp.zeros((1, tiles_here, cells), jnp.float32),
        jnp.zeros((tracers, tiles_here, cells), jnp.float32),
    )
    for sweep_index in range(lev_count - 1):
        factors, partials = eliminate(cotangent, coupling_up, coupling_down, initial)
        initial = from_behind((factors[-1], partials[-1]), "lev", 1)
    factors, partials = eliminate(cotangent, coupling_up, coupling_down, initial)
    below_field = jnp.zeros((tracers, tiles_here, cells), jnp.float32)
    for sweep_index in range(lev_count - 1):
        fields = substitute(factors, partials, below_field)
        below_field = from_behind(fields[0], "lev", -1)
    solved = substitute(factors, partials, below_field)
    weighted = solved * wet_mask[:, None]
    weighted_ext = embed(weighted)
    diffuse_ext = embed(diffusivity)[None, None]
    flow_x_ext = embed(courant_x)[:, None]
    flow_y_ext = embed(courant_y)[:, None]
    weights = stencil_weights(diffuse_ext, flow_x_ext, flow_y_ext)
    leading = weighted_ext.shape[:-1]
    spread = jnp.zeros_like(weighted_ext)
    for (shift_row, shift_col), weight in zip(stencil_offsets, weights):
        contribution = weight * weighted_ext
        offset = shift_row * padded_edge + shift_col
        if offset > 0:
            shifted = jnp.concatenate(
                [jnp.zeros(leading + (offset,), jnp.float32), contribution[..., :-offset]], axis=-1
            )
        else:
            shifted = jnp.concatenate(
                [contribution[..., -offset:], jnp.zeros(leading + (-offset,), jnp.float32)], axis=-1
            )
        spread = spread + shifted
    cycle_spots, placing = cycle_tables()
    outgoing = jnp.take(spread, jnp.asarray(cycle_spots), axis=3)
    interior = spread.reshape(leading + (padded_edge, padded_edge))[..., 1:-1, 1:-1].reshape(
        solved.shape
    )
    partners = jnp.concatenate([edge_tile, corner_tile], axis=1)

    def collect(gathered_sum, portion, first_tile):
        tile_span = portion.shape[2]
        onehot = (
            partners[:, :, None]
            == first_tile + jnp.arange(tile_span, dtype=jnp.int32)[None, None, :]
        ).astype(jnp.float32)
        return gathered_sum + jnp.einsum(
            "tkw,dnwr->dntkr", onehot, portion, precision=lax.Precision.HIGHEST
        )

    tile_count = lax.axis_size("tile")
    own_index = lax.axis_index("tile")
    reach = (2 * BAND + tiles_here - 1) // tiles_here
    fetched = collect(
        jnp.zeros((levels_here, tracers, tiles_here, 8, cycle_size), jnp.float32),
        outgoing,
        own_index * tiles_here,
    )
    for distance in range(-reach, reach + 1):
        if distance != 0:
            portion = shifted_2(outgoing, "tile", distance)
            source = (own_index - distance) % tile_count
            fetched = collect(fetched, portion, source * tiles_here)
    side_values = fetched[:, :, :, :4, : 4 * EDGE].reshape(
        levels_here, tracers, tiles_here, 4, 4, EDGE
    )
    side_choice = (
        (edge_code % 4)[:, :, None] == jnp.arange(4, dtype=jnp.int32)[None, None, :]
    ).astype(jnp.float32)
    strips = jnp.sum(side_values * side_choice[None, None, :, :, :, None], axis=4)
    strips = jnp.where((edge_code >= 4)[None, None, :, :, None], strips[..., ::-1], strips)
    corner_values = fetched[:, :, :, 4:, 4 * EDGE :]
    corner_choice = (
        corner_code[:, :, None] == jnp.arange(4, dtype=jnp.int32)[None, None, :]
    ).astype(jnp.float32)
    corner_picked = jnp.sum(corner_values * corner_choice[None, None], axis=4)
    arriving = jnp.concatenate(
        [strips.reshape(levels_here, tracers, tiles_here, 4 * EDGE), corner_picked], axis=3
    )
    returned = jnp.einsum(
        "dntr,rc->dntc", arriving, jnp.asarray(placing), precision=lax.Precision.HIGHEST
    )
    diffuse_here = diffusivity[None, None]
    return wet_mask[:, None] * ((1.0 - 5.0 * diffuse_here) * weighted + interior + returned)


PADDED = 1024
SIDE_LANES = 32
PLANE = 4
MESH = pl.DeviceIdType.MESH


def strip_selector():
    chosen = np.zeros((PADDED + 128, 256), np.float32)
    for j in range(EDGE):
        for side, lane in enumerate([PADDED - EDGE + j, EDGE * EDGE + j, EDGE * j, EDGE * j + EDGE - 1]):
            chosen[lane, SIDE_LANES * side + j] = 1.0
            chosen[lane, 128 + SIDE_LANES * side + EDGE - 1 - j] = 1.0
    for corner, cell in enumerate([0, EDGE - 1, (EDGE - 1) * EDGE, EDGE * EDGE - 1]):
        chosen[PADDED + cell % 128, SIDE_LANES * corner + EDGE] = 1.0
    return jnp.asarray(chosen, jnp.bfloat16)


def strip_placer():
    placing = np.zeros((128, PADDED), np.float32)
    for j in range(EDGE):
        for side, cell in enumerate([j, (EDGE - 1) * EDGE + j, EDGE * j, EDGE * j + EDGE - 1]):
            placing[SIDE_LANES * side + j, cell] = 1.0
    for corner, cell in enumerate([0, EDGE - 1, (EDGE - 1) * EDGE, EDGE * EDGE - 1]):
        placing[SIDE_LANES * corner + EDGE, cell] = 1.0
    return jnp.asarray(placing, jnp.bfloat16)


def split_dot(left, right):
    high = left.astype(jnp.bfloat16)
    low = (left - high.astype(jnp.float32)).astype(jnp.bfloat16)
    return jnp.dot(high, right, preferred_element_type=jnp.float32) + jnp.dot(
        low, right, preferred_element_type=jnp.float32
    )


def four_times(pair):
    return jnp.concatenate([pair, pair, pair, pair], axis=0)


def widen(rows):
    return jnp.concatenate(
        [rows, jnp.zeros((rows.shape[0], PADDED - rows.shape[1]), rows.dtype)], axis=1
    )


def solve_kernel(
    code_hbm, cot_hbm, cx_hbm, cy_hbm, dif_hbm, vd_hbm, lc_hbm, sel_hbm,
    base_ref, strips_ref, factor_ref, partial_ref, edge_ref,
    code_ref, cot_ref, cx_ref, cy_ref, dif_ref, vd_ref, lc_ref, sel_ref, sems,
):
    levels = cot_ref.shape[0]
    cells = cot_ref.shape[3]
    pairs = [
        (lc_hbm, lc_ref),
        (vd_hbm, vd_ref),
        (cot_hbm, cot_ref),
        (dif_hbm, dif_ref),
        (cx_hbm, cx_ref),
        (cy_hbm, cy_ref),
        (code_hbm, code_ref),
        (sel_hbm, sel_ref),
    ]
    copies = [
        pltpu.make_async_copy(source, target, sems.at[i])
        for i, (source, target) in enumerate(pairs)
    ]
    for copy in copies:
        copy.start()
    for copy in copies[:3]:
        copy.wait()
    depth = four_times(lc_ref[...])

    def coupling(k):
        if k == 0 or k == levels:
            return jnp.zeros((8, cells), jnp.float32)
        return jnp.where(k < depth, four_times(vd_ref[k]), 0.0)

    factor = jnp.zeros((8, cells), jnp.float32)
    partial_value = jnp.zeros((8, cells), jnp.float32)
    upper = coupling(0)
    for k in range(levels):
        lower = coupling(k + 1)
        source = jnp.concatenate([cot_ref[k, n] for n in range(4)], axis=0)
        inverse = 1.0 / ((1.0 + upper + lower) + upper * factor)
        factor = -lower * inverse
        partial_value = (source + upper * partial_value) * inverse
        factor_ref[k] = factor
        partial_ref[k] = partial_value
        upper = lower

    lane = lax.broadcasted_iota(jnp.int32, (8, PADDED), 1)
    row_lane = jnp.where(lane >= PADDED - EDGE, lane - (PADDED - EDGE), lane)
    column = lax.rem(row_lane, EDGE)
    first = column == 0
    last = column == EDGE - 1
    inside = lane < cells
    short = lax.broadcasted_iota(jnp.int32, (8, 128), 1)
    corner_0 = (short == 0) | (short == EDGE - 1)
    corner_6 = short == ((EDGE - 1) * EDGE) % 128
    corner_7 = short == (EDGE * EDGE - 1) % 128
    for copy in copies[3:6]:
        copy.wait()
    diffuse = widen(four_times(dif_ref[...]))
    quarter = 0.25 * diffuse
    centre = 1.0 - 5.0 * diffuse
    wide_depth = widen(depth)
    solved = jnp.zeros((8, cells), jnp.float32)
    for k in reversed(range(levels)):
        solved = partial_ref[k] - factor_ref[k] * solved
        u = widen(jnp.where(k < depth, solved, 0.0))
        half_x = 0.5 * widen(four_times(cx_ref[k]))
        half_y = 0.5 * widen(four_times(cy_ref[k]))
        diagonal = quarter * u
        both = pltpu.roll(diagonal, EDGE, 1) + pltpu.roll(diagonal, PADDED - EDGE, 1)
        west = both + (diffuse + half_x) * u
        east = both + (diffuse - half_x) * u
        spread = pltpu.roll((diffuse + half_y) * u, PADDED - EDGE, 1)
        spread = spread + pltpu.roll((diffuse - half_y) * u, EDGE, 1)
        spread = spread + pltpu.roll(jnp.where(first, 0.0, west), PADDED - 1, 1)
        spread = spread + pltpu.roll(jnp.where(last, 0.0, east), 1, 1)
        base_ref[k] = jnp.where(k < wide_depth, centre * u + spread, 0.0)
        edge_ref[8 * k : 8 * k + 8, :PADDED] = jnp.where(
            inside, jnp.where(first, west, east), spread
        )
        edge_ref[8 * k : 8 * k + 8, PADDED:] = (
            jnp.where(corner_0, diagonal[:, 0:128], 0.0)
            + jnp.where(corner_6, diagonal[:, 768:896], 0.0)
            + jnp.where(corner_7, diagonal[:, 896:1024], 0.0)
        )
    for copy in copies[6:]:
        copy.wait()
    both_ways = split_dot(edge_ref[...], sel_ref[...])
    parity = lax.rem(lax.broadcasted_iota(jnp.int32, (8, 128), 0), 2)
    code = jnp.zeros((8, 128), jnp.int32)
    for i in range(2):
        for side in range(4):
            code = jnp.where((parity == i) & (short // SIDE_LANES == side), code_ref[i, side], code)
    flipped = (code >= 4) & (lax.rem(short, SIDE_LANES) < EDGE)
    for k in range(levels):
        rows = both_ways[8 * k : 8 * k + 8]
        strips_ref[k] = jnp.where(flipped, rows[:, 128:], rows[:, :128])


def send_kernel(count, strips_ref, near_ref, own_sem, send_sem, recv_sem):
    chips = count // 2
    me = lax.axis_index("tile")
    chip = me // 2
    core = lax.rem(me, 2)
    place = lax.rem(chip, PLANE)

    def at(steps):
        return 2 * lax.rem(chip + steps + chips, chips) + core

    partner = me + 1 - 2 * core
    wraps = [(place + j) // PLANE for j in range(PLANE)]
    beside = [at(j - PLANE * wraps[j]) for j in range(PLANE)]
    above, below = at(PLANE), at(-PLANE)
    barrier = pltpu.get_barrier_semaphore()
    peers = [partner, above, below] + beside[1:]
    for peer in peers:
        pl.semaphore_signal(barrier, inc=1, device_id={"tile": peer}, device_id_type=MESH)
    own = pltpu.make_async_copy(strips_ref, near_ref.at[PLANE, core], own_sem)
    own.start()
    pl.semaphore_wait(barrier, len(peers))
    copies = []

    def send(source, spot, to):
        copy = pltpu.make_async_remote_copy(
            src_ref=source,
            dst_ref=near_ref.at[spot, core],
            send_sem=send_sem.at[len(copies)],
            recv_sem=recv_sem.at[spot, core],
            device_id={"tile": to},
            device_id_type=MESH,
        )
        copy.start()
        copies.append(copy)

    def arrived(spot, side):
        pltpu.make_async_remote_copy(
            src_ref=strips_ref,
            dst_ref=near_ref.at[spot, side],
            send_sem=own_sem,
            recv_sem=recv_sem.at[spot, side],
            device_id={"tile": partner},
            device_id_type=MESH,
        ).wait_recv()

    def share(spot):
        send(near_ref.at[spot, core], spot, partner)

    send(strips_ref, 0, above)
    send(strips_ref, 2 * PLANE, below)
    for j in range(1, PLANE):
        send(strips_ref, PLANE - j + PLANE * wraps[j], beside[j])
    send(strips_ref, PLANE, partner)
    for j in range(1, PLANE):
        spot = PLANE + j - PLANE * wraps[j]
        arrived(spot, core)
        share(spot)
    arrived(0, core)
    arrived(2 * PLANE, core)
    for j in range(1, PLANE):
        source = near_ref.at[2 * PLANE - 2 * PLANE * wraps[j], core]
        send(source, 2 * PLANE - PLANE * wraps[j] - j, beside[j])
    share(0)
    share(2 * PLANE)
    for j in range(1, PLANE):
        spot = j + PLANE * wraps[j]
        arrived(spot, core)
        share(spot)
    for spot in range(2 * PLANE + 1):
        arrived(spot, 1 - core)
    own.wait()
    for copy in copies:
        copy.wait_send()


def place_kernel(
    count, et_ref, ec_ref, ct_ref, cc_ref, near_ref, base_ref, lc_ref, place_ref,
    out_ref, arriving_ref,
):
    levels = base_ref.shape[0]
    cells = out_ref.shape[3]
    me = lax.axis_index("tile")
    lane = lax.broadcasted_iota(jnp.int32, (8, 128), 1)
    parity = lax.rem(lax.broadcasted_iota(jnp.int32, (8, 128), 0), 2)
    group = lane // SIDE_LANES
    spot = lax.rem(lane, SIDE_LANES)
    total = jnp.zeros((levels, 8, 128), jnp.float32)
    for i in range(2):
        for tiles_ref, codes_ref, wanted in (
            (et_ref, ec_ref, spot < EDGE),
            (ct_ref, cc_ref, spot == EDGE),
        ):
            for side in range(4):
                tile = tiles_ref[i, side]
                there = jnp.maximum(tile, 0)
                slot = lax.rem(there // 4 - me // 2 + PLANE + count // 2, count // 2)
                slot = jnp.where(tile < 0, 0, slot)
                values = near_ref[slot, lax.rem(there // 2, 2)]
                values = jnp.where(
                    lax.rem(there, 2) == i, values, pltpu.roll(values, 1 if i == 1 else 7, 1)
                )
                shift = lax.rem(SIDE_LANES * (side - lax.rem(codes_ref[i, side], 4)) + 128, 128)
                values = pltpu.roll(values, shift, 2)
                chosen = wanted & (group == side) & (parity == i) & (tile >= 0)
                total = jnp.where(chosen[None], values, total)
    for k in range(levels):
        arriving_ref[8 * k : 8 * k + 8] = total[k]
    returned = split_dot(arriving_ref[...], place_ref[...])
    depth = four_times(lc_ref[...])
    for k in range(levels):
        result = base_ref[k][:, :cells] + jnp.where(
            k < depth, returned[8 * k : 8 * k + 8, :cells], 0.0
        )
        for n in range(4):
            out_ref[k, n] = result[2 * n : 2 * n + 2]


def shards_fast(
    cotangent,
    courant_x,
    courant_y,
    diffusivity,
    vert_diff,
    level_count,
    edge_tile,
    edge_code,
    corner_tile,
    corner_code,
):
    levels, tracers, tiles_here, cells = cotangent.shape
    count = lax.axis_size("tile")
    vmem = pl.BlockSpec(memory_space=pltpu.VMEM)
    smem = pl.BlockSpec(memory_space=pltpu.SMEM)
    hbm = pl.BlockSpec(memory_space=pltpu.HBM)
    base, strips = pl.pallas_call(
        solve_kernel,
        name="solve",
        out_shape=(
            jax.ShapeDtypeStruct((levels, 8, PADDED), jnp.float32),
            jax.ShapeDtypeStruct((levels, 8, 128), jnp.float32),
        ),
        in_specs=[hbm] * 8,
        out_specs=(vmem, vmem),
        scratch_shapes=[
            pltpu.VMEM((levels, 8, cells), jnp.float32),
            pltpu.VMEM((levels, 8, cells), jnp.float32),
            pltpu.VMEM((8 * levels, PADDED + 128), jnp.float32),
            pltpu.SMEM(edge_code.shape, jnp.int32),
            pltpu.VMEM(cotangent.shape, jnp.float32),
            pltpu.VMEM(courant_x.shape, jnp.float32),
            pltpu.VMEM(courant_y.shape, jnp.float32),
            pltpu.VMEM(diffusivity.shape, jnp.float32),
            pltpu.VMEM(vert_diff.shape, jnp.float32),
            pltpu.VMEM(level_count.shape, jnp.int32),
            pltpu.VMEM((PADDED + 128, 256), jnp.bfloat16),
            pltpu.SemaphoreType.DMA((8,)),
        ],
        compiler_params=pltpu.CompilerParams(vmem_limit_bytes=62 << 20),
    )(edge_code, cotangent, courant_x, courant_y, diffusivity, vert_diff, level_count, strip_selector())
    near = pl.pallas_call(
        functools.partial(send_kernel, count),
        name="send",
        out_shape=jax.ShapeDtypeStruct((2 * PLANE + 1, 2, levels, 8, 128), jnp.float32),
        in_specs=[hbm],
        out_specs=hbm,
        scratch_shapes=[
            pltpu.SemaphoreType.DMA,
            pltpu.SemaphoreType.DMA((4 * PLANE + 1,)),
            pltpu.SemaphoreType.DMA((2 * PLANE + 1, 2)),
        ],
        compiler_params=pltpu.CompilerParams(collective_id=0, has_side_effects=True),
    )(strips)
    return pl.pallas_call(
        functools.partial(place_kernel, count),
        name="place",
        out_shape=jax.ShapeDtypeStruct(cotangent.shape, jnp.float32),
        in_specs=[smem] * 4 + [vmem] * 4,
        out_specs=vmem,
        scratch_shapes=[pltpu.VMEM((8 * levels, 128), jnp.float32)],
        compiler_params=pltpu.CompilerParams(vmem_limit_bytes=40 << 20),
    )(edge_tile, edge_code, corner_tile, corner_code, near, base, level_count, strip_placer())


def solution(mesh):
    placed = (
        P("lev", None, "tile", None),
        P("lev", "tile", None),
        P("lev", "tile", None),
        P("tile", None),
        P("lev", "tile", None),
        P("tile", None),
        P("tile", None),
        P("tile", None),
        P("tile", None),
        P("tile", None),
    )
    fast = mesh.shape["lev"] == 1 and mesh.shape["tile"] % 8 == 0 and mesh.shape["tile"] > 2 * BAND
    return jax.shard_map(
        shards_fast if fast else shards, mesh=mesh, in_specs=placed, out_specs=P("lev", None, "tile", None), check_vma=False
    )
```
